128 devices in a mesh: seq: 16 (over x, z), exp: 8 (over y, core).
Axes of the slice: x: 4, y: 4, z: 4, core: 2. Of those that a mesh axis runs over, the one named last changes fastest.
Arguments:
- hidden: bfloat16 [16384, 2048], P('seq'), may hold values from -9 to 9
- mixer_gain: float32 [2048], replicated, may hold values from 0.1 to 1.9
- gate_proj: bfloat16 [2048, 4096], P(None, 'exp'), may hold values from -0.125 to 0.125
- value_proj: bfloat16 [2048, 4096], P(None, 'exp'), may hold values from -0.125 to 0.125
- state_proj: bfloat16 [2048, 2048], P(None, 'exp'), may hold values from -0.125 to 0.125
- log_decay: float32 [16384, 64], P('seq', 'exp'), may hold values from -0.8 to 0
- step_size: float32 [16384, 64], P('seq', 'exp'), may hold values from 0 to 0.25
- skip_gain: float32 [64], P('exp'), may hold values from 0.5 to 1.5
- group_gain: float32 [4096], P('exp'), may hold values from 0.1 to 1.9
- out_proj: bfloat16 [4096, 2048], P('exp'), may hold values from -0.09375 to 0.09375
- moe_gain: float32 [2048], replicated, may hold values from 0.1 to 1.9
- router: bfloat16 [2048, 128], replicated, may hold values from -0.0625 to 0.0625
- expert_ids: int32 [16384, 8], P(('seq', 'exp')), may hold values from 0 to 127, all different within a row; in each aligned block of 128 rows (0 to 127, 128 to 255, ...) at most 12 rows name the same one
- expert_gate_up: bfloat16 [128, 2048, 1536], P(('seq', 'exp')), may hold values from -0.125 to 0.125
- expert_down: bfloat16 [128, 768, 2048], P(('seq', 'exp')), may hold values from -0.4375 to 0.4375
Outputs:
- mixer_out: bfloat16 [16384, 2048], P(('seq', 'exp'))
- layer_out: bfloat16 [16384, 2048], P(('seq', 'exp'))
The draws below stay inside these ranges and needn't reach their ends.
Inputs may be any that keep to these rules, and one draw needn't show every extreme that they name: `expert_ids`: within the 128 rows of one device (aligned blocks) no expert is named more than 12 times, and in some blocks some expert is named exactly 12 times; a row never names an expert twice.
All inputs are finite; a program needn't handle non-finite values.
Results may differ from the reference program's by a relative error of at most 0.025.
Values may be sent and summed in bfloat16 or wider, within the bound.
No kernel may reach another device: no remote copies, remote signals or barrier semaphores. Data moves between devices by JAX's collectives and lax.ppermute only.
A program may use at most 128 MiB of HBM per device.

```python
import math
import jax
import jax.numpy as jnp
import numpy as np
from jax import lax

D = 2048
H = 64
P_SIZE = 64
N = 128
G = 8
Q = 256
F = 768
TOP = 8
TOKENS_PER_SHARD = 128
SHARD = 1024
SEQUENCE_TOKENS = 16384
EXPERTS = 128
CAP = 12
N_SEQ = 16
N_EXP = 8


def decay_parts(key):
    base_key = jax.random.fold_in(key, 7331)
    keys = jax.random.split(base_key, 7)
    share = 0.5
    fast = jax.random.uniform(keys[0], (H,)) < share
    fast_rate = jnp.exp(jax.random.uniform(keys[1], (H,), minval=jnp.log(1.0 / 50.0), maxval=jnp.log(1.0 / 30.0)))
    slow_rate = jax.random.uniform(keys[2], (H,), minval=0.2, maxval=0.6) / SEQUENCE_TOKENS
    base_rate = jnp.where(fast, fast_rate, slow_rate)
    shard_factor = jnp.exp(jax.random.uniform(keys[3], (SEQUENCE_TOKENS // SHARD, H), minval=jnp.log(0.5), maxval=jnp.log(2.0)))
    shard_factor = jnp.repeat(shard_factor, SHARD, axis=0)
    rough = jax.random.uniform(keys[4], (SEQUENCE_TOKENS, H), minval=0.5, maxval=1.5)
    decay_rates = base_rate[None, :] * shard_factor * rough
    slot_positions = jax.random.randint(keys[5], (2,), 0, SEQUENCE_TOKENS)
    outbound_rows = jnp.any(jnp.arange(SEQUENCE_TOKENS)[:, None] == slot_positions[None, :], axis=1)
    kept_mask = jax.random.uniform(keys[6], (SEQUENCE_TOKENS, H), minval=0.5, maxval=0.8)
    log_decay_rates = -decay_rates + jnp.where(outbound_rows[:, None], jnp.log(kept_mask), 0.0)
    return (decay_rates, log_decay_rates)


def draw_log_decay(key, part):
    decay_rates, log_decay_rates = decay_parts(key)
    return log_decay_rates.astype(jnp.float32)


def draw_step_size(key, part):
    decay_rates, log_decay_rates = decay_parts(key)
    noise = jax.random.uniform(jax.random.fold_in(key, 99), (SEQUENCE_TOKENS, H), minval=0.5, maxval=1.5)
    return (jnp.sqrt(2.0 * decay_rates / N) * noise).astype(jnp.float32)


def draw_hidden(key, part):
    keys = jax.random.split(jax.random.fold_in(key, 4242), 3)
    columns = jnp.exp(jax.random.uniform(keys[1], (1, D), minval=jnp.log(0.15), maxval=jnp.log(1.5)))
    rows_scale = jnp.exp(jax.random.uniform(keys[2], (SEQUENCE_TOKENS, 1), minval=jnp.log(0.5), maxval=jnp.log(2.0)))
    base = jnp.clip(jax.random.normal(keys[0], (SEQUENCE_TOKENS, D)), -3.0, 3.0)
    return (base * columns * rows_scale).astype(jnp.bfloat16)


def shard_levels(rng, dims, cuts, smallest, high):
    level, own = 1.0, jax.random.fold_in(rng, 6)
    for dim, shards_of in cuts:
        draws = jnp.exp(jax.random.uniform(jax.random.fold_in(own, dim), (shards_of,), jnp.float32, smallest / len(cuts), high / len(cuts)))
        level = level * jnp.repeat(draws, dims[dim] // shards_of).reshape([-1 if axis == dim else 1 for axis in range(len(dims))])
    return level


def deal_out(own_key, own, number, rows, number_of, top, most, slope):
    order = jax.random.permutation(own_key, number_of)
    packed, usual = load_shares(number_of, rows * top, most, slope, True), load_shares(number_of, rows * top, most, slope, False)
    places = jnp.arange(number_of)

    def named(sizes, turn):
        used = int((sizes > 0).sum())
        fixed = max(1, used // 4)
        moved = fixed + (places - fixed + turn * (used - fixed)) % max(1, number_of - fixed)
        return jnp.zeros((number_of,), jnp.int32).at[order[jnp.where(places < fixed, places, moved)]].set(jnp.asarray(sizes, jnp.int32))

    sizes = jnp.where(number % 4 == 0, named(packed, number // 4), named(usual, number - number // 4 - 1))
    mixed = jax.random.permutation(jax.random.fold_in(own, 3), number_of)
    source_of, sink = mixed[0:number_of // 2 * 2:2], mixed[1:number_of // 2 * 2:2]
    slack = jnp.minimum(sizes[source_of] - 1, most - sizes[sink]) // 2
    slack = jnp.where((source_of == order[0]) | (sink == order[0]) | (sizes[sink] == 0), 0, jnp.maximum(slack, 0))
    moved = jax.random.randint(jax.random.fold_in(own, 4), (number_of // 2,), 0, 1 << 20) % (slack + 1)
    sizes = sizes.at[source_of].add(-moved).at[sink].add(moved)
    members = jnp.searchsorted(jnp.cumsum(sizes), jnp.arange(rows * top), side="right").astype(jnp.int32)
    listing = members.reshape(top, rows).T
    listing = listing[jax.random.permutation(jax.random.fold_in(own, 1), rows)]
    turn = jax.random.randint(jax.random.fold_in(own, 2), (rows, 1), 0, top)
    return jnp.take_along_axis(listing, (jnp.arange(top)[None, :] + turn) % top, axis=1)


def load_shares(count, total, bound, slope, full):
    loads = [(1 << 20) // math.isqrt(rank ** slope) + 1 for rank in range(1, count + 1)]
    largest = bound if full else min(bound, max(-(-total // count), total * loads[0] // sum(loads)))
    least = 1 if total - largest >= count - 1 else 0
    counts, rest = [largest] + [least] * (count - 1), total - largest - least * (count - 1)
    while rest > 0:
        candidates = [i for i in range(1, count) if counts[i] < largest] or [i for i in range(1, count) if counts[i] < bound]
        mass, left = sum([loads[i] for i in candidates]), rest
        for i in candidates:
            addition = min(bound - counts[i], max(1, left * loads[i] // mass), rest)
            counts[i] = counts[i] + addition
            rest = rest - addition
    return np.array(counts)


def scatter_about(stream_key, dims, deviation, most, shards=(), kind=jnp.bfloat16):
    factor_of = shard_levels(stream_key, dims, shards, -0.22, 0.18) if shards else 1.0
    array = jax.random.normal(stream_key, dims, jnp.float32) * deviation * factor_of
    return jnp.minimum(jnp.maximum(array, -most), most).astype(kind)


def setup_inputs(seed: int = 0) -> dict:
    key_of = jax.random.split(jax.random.key(seed), 16)
    hidden = draw_hidden(jax.random.fold_in(key_of[15], 71), 0)
    mixer_gain = jnp.clip(1.0 + 0.18 * jax.random.normal(key_of[1], (D,), jnp.float32), 0.1, 1.9)
    gate_proj = scatter_about(key_of[2], (D, H * P_SIZE), D ** -0.5, 0.125, ((1, 8),))
    value_proj = scatter_about(key_of[3], (D, H * P_SIZE), D ** -0.5, 0.125, ((1, 8),))
    state_proj = scatter_about(key_of[4], (D, 2 * G * N), D ** -0.5, 0.125, ((1, 8),))
    log_decay = draw_log_decay(jax.random.fold_in(key_of[15], 71), 0)
    step_size = draw_step_size(jax.random.fold_in(key_of[15], 71), 0)
    skip_gain = jnp.clip(0.5 + 1.0 * jax.random.uniform(key_of[7], (H,), jnp.float32) ** shard_levels(key_of[7], (H,), ((0, 8),), -0.2, 0.2), 0.5, 1.5)
    group_gain = jnp.clip(1.0 + 0.18 * jax.random.normal(key_of[8], (H * P_SIZE,), jnp.float32), 0.1, 1.9)
    out_proj = scatter_about(key_of[9], (H * P_SIZE, D), (H * P_SIZE) ** -0.5, 0.09375, ((0, 8),))
    moe_gain = jnp.clip(1.0 + 0.18 * jax.random.normal(key_of[10], (D,), jnp.float32), 0.1, 1.9)
    router = scatter_about(key_of[11], (D, EXPERTS), (4 * D) ** -0.5, 0.0625)
    expert_ids_keys = jax.random.split(jax.random.fold_in(key_of[12], 1), SEQUENCE_TOKENS // TOKENS_PER_SHARD)
    expert_ids_turns = jax.random.permutation(jax.random.fold_in(key_of[12], 3), SEQUENCE_TOKENS // TOKENS_PER_SHARD)
    expert_ids = jax.vmap(lambda own, number: deal_out(jax.random.fold_in(key_of[12], 2), own, number, TOKENS_PER_SHARD, EXPERTS, TOP, CAP, 2))(expert_ids_keys, expert_ids_turns).reshape((SEQUENCE_TOKENS, TOP))
    expert_gate_up = scatter_about(key_of[13], (EXPERTS, D, 2 * F), D ** -0.5, 0.125, ((0, 128),))
    expert_down = scatter_about(key_of[14], (EXPERTS, F, D), (F // 4) ** -0.5, 0.4375, ((0, 128),))
    return {"hidden": hidden, "mixer_gain": mixer_gain, "gate_proj": gate_proj, "value_proj": value_proj, "state_proj": state_proj, "log_decay": log_decay, "step_size": step_size, "skip_gain": skip_gain, "group_gain": group_gain, "out_proj": out_proj, "moe_gain": moe_gain, "router": router, "expert_ids": expert_ids, "expert_gate_up": expert_gate_up, "expert_down": expert_down}


epsilon = 1e-05
highest = lax.Precision.HIGHEST

def rms_rows(values, gain):
    wide = values.astype(jnp.float32)
    inv_scale = lax.rsqrt(lax.optimization_barrier(jnp.mean(wide * wide, axis=-1, keepdims=True)) + epsilon)
    return (wide * inv_scale * gain).astype(jnp.bfloat16)

def block_terms(out_maps, in_maps, inputs, log_decay_rates):
    block_len = log_decay_rates.shape[1]
    cumulative = jnp.cumsum(log_decay_rates, axis=1)
    lower_tri = jnp.arange(block_len)[:, None] >= jnp.arange(block_len)[None, :]
    gap_matrix = cumulative[:, :, None] - cumulative[:, None, :]
    decay_mask = jnp.exp(jnp.where(lower_tri[None, :, :, None, None], gap_matrix, -jnp.inf))
    scores = jnp.einsum('ctgn,csgn->ctsg', out_maps, in_maps, precision=highest)
    weights = scores[..., None] * decay_mask
    within = jnp.einsum('ctsgj,csgjp->ctgjp', weights, inputs, precision=highest)
    block_end = cumulative[:, -1]
    to_end = jnp.exp(block_end[:, None] - cumulative)
    states = jnp.einsum('csgn,csgjp->cgjnp', in_maps, inputs * to_end[..., None], precision=highest)
    return (cumulative, within, states, block_end)

def reference(hidden, mixer_gain, gate_proj, value_proj, state_proj, log_decay, step_size, skip_gain, group_gain, out_proj, moe_gain, router, expert_ids, expert_gate_up, expert_down):
    heads_in = H // G
    blocks = SEQUENCE_TOKENS // Q
    mixer_in = rms_rows(hidden, mixer_gain)
    gate_act = jnp.dot(mixer_in, gate_proj, preferred_element_type=jnp.float32).astype(jnp.bfloat16)
    value_act = jnp.dot(mixer_in, value_proj, preferred_element_type=jnp.float32).astype(jnp.bfloat16)
    state_act = jnp.dot(mixer_in, state_proj, preferred_element_type=jnp.float32).astype(jnp.bfloat16)
    maps_all = state_act.astype(jnp.float32).reshape(blocks, Q, G, 2, N)
    in_all = maps_all[:, :, :, 0]
    out_all = maps_all[:, :, :, 1]
    head_values = value_act.astype(jnp.float32).reshape(blocks, Q, G, heads_in, P_SIZE)
    log_decay_rates = log_decay.reshape(blocks, Q, G, heads_in)
    head_inputs = head_values * step_size.reshape(blocks, Q, G, heads_in)[..., None]

    def advance(carry_state, segment):
        out_maps, in_maps, inputs, decay_rates = segment
        cumulative, within, states, block_end = block_terms(out_maps[None], in_maps[None], inputs[None], decay_rates[None])
        carried = jnp.exp(cumulative)[..., None] * jnp.einsum('ctgn,gjnp->ctgjp', out_maps[None], carry_state, precision=highest)
        next_state = jnp.exp(block_end[0])[..., None, None] * carry_state + states[0]
        return (next_state, (within + carried)[0])
    start_state = jnp.zeros((G, heads_in, N, P_SIZE), jnp.float32)
    _, mixer_heads = lax.scan(advance, start_state, (out_all, in_all, head_inputs, log_decay_rates))
    mixer_heads = mixer_heads.reshape(SEQUENCE_TOKENS, G, heads_in, P_SIZE) + skip_gain.reshape(G, heads_in)[:, :, None] * head_values.reshape(SEQUENCE_TOKENS, G, heads_in, P_SIZE)
    gated = mixer_heads.reshape(SEQUENCE_TOKENS, G, heads_in * P_SIZE) * jax.nn.silu(gate_act.astype(jnp.float32)).reshape(SEQUENCE_TOKENS, G, heads_in * P_SIZE)
    normed = gated * lax.rsqrt(lax.optimization_barrier(jnp.mean(gated * gated, axis=-1, keepdims=True)) + epsilon)
    normed_mix = (normed.reshape(SEQUENCE_TOKENS, H * P_SIZE) * group_gain).astype(jnp.bfloat16)
    span = H * P_SIZE // N_EXP
    head_sum = jnp.zeros((SEQUENCE_TOKENS, D), jnp.float32)
    for position in range(N_EXP):
        partial_value = jnp.dot(normed_mix[:, position * span:(position + 1) * span], out_proj[position * span:(position + 1) * span], preferred_element_type=jnp.float32)
        head_sum = head_sum + lax.optimization_barrier(partial_value.astype(jnp.bfloat16)).astype(jnp.float32)
    mixer_out = (hidden.astype(jnp.float32) + head_sum).astype(jnp.bfloat16)
    expert_input = rms_rows(mixer_out, moe_gain)
    affinity = jax.nn.sigmoid(jnp.dot(expert_input, router, preferred_element_type=jnp.float32))
    chosen = expert_ids[:, :, None] == jnp.arange(EXPERTS).astype(jnp.int32)[None, None, :]
    picked = lax.optimization_barrier(jnp.sum(jnp.where(chosen, affinity[:, None, :], 0.0), axis=-1))
    route_weight = picked / lax.optimization_barrier(jnp.sum(picked, axis=-1, keepdims=True))
    devices = N_SEQ * N_EXP
    flat_ids = expert_ids.reshape(devices, TOKENS_PER_SHARD * TOP)
    onehot = (flat_ids[..., None] == jnp.arange(EXPERTS).astype(jnp.int32)).astype(jnp.int32)
    rank_index = lax.optimization_barrier(jnp.sum((jnp.cumsum(onehot, axis=1) - onehot) * onehot, axis=-1)).astype(jnp.int32)
    slot_index = (jnp.arange(devices).astype(jnp.int32)[:, None] * CAP + rank_index).astype(jnp.int32)
    token_index = (jnp.arange(devices).astype(jnp.int32)[:, None] * TOKENS_PER_SHARD + jnp.arange(TOKENS_PER_SHARD * TOP).astype(jnp.int32)[None, :] // TOP).astype(jnp.int32)
    slot_table = jnp.full((EXPERTS, devices * CAP), SEQUENCE_TOKENS, jnp.int32)
    slot_table = slot_table.at[flat_ids.reshape(-1), slot_index.reshape(-1)].set(token_index.reshape(-1))
    padded = jnp.concatenate([expert_input, jnp.zeros((1, D), jnp.bfloat16)], axis=0)

    def expert(segment):
        row_index, gate_up, down_rows = segment
        row_piece = padded[row_index]
        projected = jnp.dot(row_piece, gate_up, preferred_element_type=jnp.float32)
        activated = (jax.nn.silu(projected[:, :F]) * projected[:, F:]).astype(jnp.bfloat16)
        return jnp.dot(activated, down_rows, preferred_element_type=jnp.float32).astype(jnp.bfloat16)
    results = lax.map(expert, (slot_table, expert_gate_up, expert_down))
    ids_rows = flat_ids.reshape(SEQUENCE_TOKENS, TOP)
    slots_rows = slot_index.reshape(SEQUENCE_TOKENS, TOP)
    total = mixer_out.astype(jnp.float32)
    for position in range(TOP):
        fetched = results[ids_rows[:, position], slots_rows[:, position]]
        total = total + fetched.astype(jnp.float32) * route_weight[:, position:position + 1]
    layer_out = total.astype(jnp.bfloat16)
    return (mixer_out, layer_out)
```

```python
import jax
import jax.numpy as jnp
from jax import lax
from jax.experimental import pallas as pl
from jax.experimental.pallas import tpu as pltpu
from jax.sharding import PartitionSpec as P

D = 2048
HALF = D // 2
P_SIZE = 64
N = 128
Q = 256
F = 768
CAP = 12
SLAB = 2 * CAP

f32 = jnp.float32
bf16 = jnp.bfloat16
epsilon = 1e-05
highest = lax.Precision.HIGHEST
VMEM_LIMIT = 50 * 2**20


def params():
    return pltpu.CompilerParams(
        dimension_semantics=("arbitrary",), vmem_limit_bytes=VMEM_LIMIT
    )


def cost(flops, nbytes, transcendentals=0):
    return pl.CostEstimate(
        flops=int(flops), bytes_accessed=int(nbytes), transcendentals=int(transcendentals)
    )


def iota(shape, axis, kind=jnp.int32):
    return lax.broadcasted_iota(jnp.int32, shape, axis).astype(kind)


def dot(a, b):
    return jnp.dot(a, b, preferred_element_type=f32)


def dot_first(a, b):
    return lax.dot_general(a, b, (((0,), (0,)), ((), ())), preferred_element_type=f32)


def dot_last(a, b):
    return lax.dot_general(a, b, (((1,), (1,)), ((), ())), preferred_element_type=f32)


def running_sum(rows):
    count = rows.shape[0]
    lower = (iota((count, count), 0) >= iota((count, count), 1)).astype(f32)
    return jnp.dot(lower, rows, precision=highest, preferred_element_type=f32)


def per_channel(values):
    heads = values.shape[1]
    lanes = heads * P_SIZE
    first = iota((heads, lanes), 0) * P_SIZE
    lane = iota((heads, lanes), 1)
    spread = ((lane >= first) & (lane < first + P_SIZE)).astype(f32).astype(bf16)
    coarse = values.astype(bf16)
    fine = (values - coarse.astype(f32)).astype(bf16)
    return dot(coarse, spread) + dot(fine, spread)


def row_per_channel(row):
    return per_channel(jnp.broadcast_to(row, (8, row.shape[1])))[0:1]


def local_state_kernel(
    hidden_ref,
    gain_ref,
    value_ref,
    state_ref,
    decay_ref,
    step_ref,
    mixed_ref,
    x_ref,
    maps_ref,
    enter_ref,
    sent_ref,
    state,
    total,
):
    block = pl.program_id(0)

    @pl.when(block == 0)
    def _():
        state[...] = jnp.zeros_like(state)
        total[...] = jnp.zeros_like(total)

    wide = hidden_ref[...].astype(f32)
    scale = lax.rsqrt(jnp.mean(wide * wide, axis=-1, keepdims=True) + epsilon)
    mixed = (wide * scale * gain_ref[...]).astype(bf16)
    mixed_ref[...] = mixed
    x = dot(mixed, value_ref[...]).astype(bf16)
    x_ref[...] = x
    maps = dot(mixed, state_ref[...]).astype(bf16)
    maps_ref[...] = maps
    sums = running_sum(decay_ref[...])
    end = sums[Q - 1 : Q]
    weight = per_channel(jnp.exp(end - sums) * step_ref[...])
    weighted = (x.astype(f32) * weight).astype(bf16)
    old = state[...]
    enter_ref[0] = old.astype(bf16)
    new = old * row_per_channel(jnp.exp(end)) + dot_first(maps[:, :N], weighted)
    state[...] = new
    total[0:1, :] = total[0:1, :] + end

    @pl.when(block == pl.num_programs(0) - 1)
    def _():
        parts = sent_ref.shape[0]
        channels = new.shape[1]
        log_total = row_per_channel(total[0:1, :])
        coarse = log_total.astype(bf16).astype(f32)
        which = iota((8, channels), 0)
        tail = jnp.where(which == 0, coarse, jnp.where(which == 1, log_total - coarse, 0.0))
        rows = new.reshape(parts, N // parts, channels)
        sent_ref[...] = jnp.concatenate(
            [rows, jnp.broadcast_to(tail[None], (parts, 8, channels))], axis=1
        ).astype(bf16)


def prefix_kernel(got_ref, out_ref):
    count = got_ref.shape[0]
    rows = out_ref.shape[1]
    carry = jnp.zeros(out_ref.shape[1:], f32)
    for shard in range(count):
        out_ref[shard] = carry.astype(bf16)
        got = got_ref[shard].astype(f32)
        decay = jnp.exp(got[rows : rows + 1] + got[rows + 1 : rows + 2])
        carry = decay * carry + got[:rows]


def within_kernel(
    mixed_ref, gate_w_ref, x_ref, maps_ref, decay_ref, step_ref, gate_ref, within_ref
):
    gate_ref[...] = dot(mixed_ref[...], gate_w_ref[...]).astype(bf16)
    sums = running_sum(decay_ref[...])
    heads = sums.shape[1]
    blank = jnp.zeros((Q, 128 - 2 * heads), f32)
    across = jnp.concatenate([sums, step_ref[...], blank], axis=1).T
    maps = maps_ref[...]
    scores = dot_last(maps[:, N:], maps[:, :N])
    scores = jnp.where(iota((Q, Q), 0) >= iota((Q, Q), 1), scores, 0.0)
    causal = iota((Q, Q), 0) >= iota((Q, Q), 1)
    left = (iota((Q, 2 * P_SIZE), 1) < P_SIZE).astype(f32).astype(bf16)
    right = (iota((Q, 2 * P_SIZE), 1) >= P_SIZE).astype(f32).astype(bf16)
    for pair in range(heads // 2):
        weights = []
        for head in (2 * pair, 2 * pair + 1):
            gap = sums[:, head : head + 1] - across[head : head + 1]
            decay = jnp.exp(jnp.where(causal, gap, -1e30))
            weights.append(
                (scores * decay * across[heads + head : heads + head + 1]).astype(bf16)
            )
        lanes = slice(pair * 2 * P_SIZE, (pair + 1) * 2 * P_SIZE)
        x = x_ref[:, lanes]
        within_ref[:, lanes] = dot(
            jnp.concatenate(weights, axis=1), jnp.concatenate([x * left, x * right], axis=0)
        )


def normed_kernel(
    core_ref,
    within_ref,
    x_ref,
    maps_ref,
    gate_ref,
    decay_ref,
    enter_ref,
    incoming_ref,
    skip_ref,
    gain_ref,
    own_ref,
    other_ref,
    before,
):
    block = pl.program_id(0)

    @pl.when(block == 0)
    def _():
        before[...] = jnp.zeros_like(before)

    passed = before[0:1, :]
    sums = running_sum(decay_ref[...])
    entering = enter_ref[0].astype(f32) + row_per_channel(jnp.exp(passed)) * incoming_ref[
        ...
    ].astype(f32)
    before[0:1, :] = passed + sums[Q - 1 : Q]
    carried = per_channel(jnp.exp(sums)) * dot(maps_ref[:, N:], entering.astype(bf16))
    heads = within_ref[...] + carried + row_per_channel(skip_ref[...]) * x_ref[...].astype(f32)
    gate = gate_ref[...].astype(f32)
    gated = heads * (gate * jax.nn.sigmoid(gate))
    scale = lax.rsqrt(jnp.mean(gated * gated, axis=-1, keepdims=True) + epsilon)
    normed = gated * scale * gain_ref[...]
    rows = own_ref.shape[0]
    first, second = normed[:rows], normed[rows:]
    mine = core_ref[0] == 0
    own_ref[...] = jnp.where(mine, first, second).astype(bf16)
    other_ref[...] = jnp.where(mine, second, first).astype(bf16)


def project_kernel(where_ref, own_ref, got_ref, own_w_ref, got_w_ref, out_ref):
    out_ref[...] = (
        dot(own_ref[...], own_w_ref[...]) + dot(got_ref[...], got_w_ref[...])
    ).astype(bf16)


def slots(row):
    place = row - SLAB * jnp.floor((row + 0.5) * (1.0 / SLAB))
    slot = jnp.where(place < 8, place, jnp.where(place < 20, place - 8, place - 12))
    second = ((place >= 8) & (place < 16)) | (place >= 20)
    return slot, second


def expert_of(block, rows, experts):
    gap = iota((rows, experts), 0) + block * rows - SLAB * iota((rows, experts), 1)
    return ((gap >= 0) & (gap < SLAB)).astype(f32).astype(bf16)


def dispatch_kernel(
    where_ref,
    a_ref,
    b_ref,
    c_ref,
    d_ref,
    hidden_ref,
    gain_ref,
    router_ref,
    ids_ref,
    mixer_ref,
    rank_ref,
    weight_ref,
    out_ref,
    rows_in,
    ranks,
):
    block = pl.program_id(0)
    experts = router_ref.shape[1]
    tokens = ids_ref.shape[0]

    @pl.when(block == 0)
    def _():
        head_sum = (
            a_ref[...].astype(f32)
            + b_ref[...].astype(f32)
            + c_ref[...].astype(f32)
            + d_ref[...].astype(f32)
        )
        mixer_out = (hidden_ref[...].astype(f32) + head_sum).astype(bf16)
        mixer_ref[...] = mixer_out
        wide = mixer_out.astype(f32)
        scale = lax.rsqrt(jnp.mean(wide * wide, axis=-1, keepdims=True) + epsilon)
        expert_input = (wide * scale * gain_ref[...]).astype(bf16)
        rows_in[:tokens, :] = expert_input[:, :HALF]
        rows_in[tokens:, :] = expert_input[:, HALF:]
        affinity = jax.nn.sigmoid(dot(expert_input, router_ref[...]))
        lane = iota((tokens, experts), 1)
        named = jnp.zeros((tokens, experts), f32)
        for k in range(ids_ref.shape[1]):
            named = named + (ids_ref[:, k : k + 1] == lane).astype(f32)
        picked = named * affinity
        weight_ref[...] = picked / jnp.sum(picked, axis=-1, keepdims=True)
        earlier = (iota((tokens, tokens), 0) > iota((tokens, tokens), 1)).astype(f32)
        rank = dot(earlier.astype(bf16), named.astype(bf16))
        rank = jnp.where(named > 0.5, rank, -1.0)
        rank_ref[...] = rank
        ranks[...] = rank.astype(bf16)

    rows = out_ref.shape[0]
    ranked = dot_last(expert_of(block, rows, experts), ranks[...])
    slot, second = slots(iota((rows, tokens), 0, f32))
    hit = ranked == slot
    first_half = (hit & jnp.logical_not(second)).astype(f32).astype(bf16)
    second_half = (hit & second).astype(f32).astype(bf16)
    picker = jnp.concatenate([first_half, second_half], axis=1)
    out_ref[...] = dot(picker, rows_in[...]).astype(bf16)


def expert_kernel(a_ref, b_ref, c_ref, up_ref, down_ref, out_ref):
    peers = a_ref.shape[0]
    rows = peers * 8
    part = rows // 2
    place = iota((rows, rows), 0)
    lane = iota((rows, rows), 1)

    def source(row):
        inner = row & (part - 1)
        return ((inner >> 2) << 3) + jnp.where(row >= part, 4, 0) + (inner & 3)

    apart = (source(place) == lane).astype(f32).astype(bf16)
    together = (place == source(lane)).astype(f32).astype(bf16)
    tail = dot(apart, c_ref[...].reshape(rows, HALF)).astype(bf16)
    x0 = jnp.concatenate([a_ref[...].reshape(rows, HALF), tail[:part]], axis=0)
    x1 = jnp.concatenate([b_ref[...].reshape(rows, HALF), tail[part:]], axis=0)
    projected = dot(x0, up_ref[0, :HALF]) + dot(x1, up_ref[0, HALF:])
    gate = projected[:, :F]
    hidden = (gate * jax.nn.sigmoid(gate) * projected[:, F:]).astype(bf16)
    y0 = dot(hidden, down_ref[0, :, :HALF]).astype(bf16)
    y1 = dot(hidden, down_ref[0, :, HALF:]).astype(bf16)
    out_ref[:, 0] = y0[:rows].reshape(peers, 8, HALF)
    out_ref[:, 1] = y1[:rows].reshape(peers, 8, HALF)
    tail = jnp.concatenate([y0[rows:], y1[rows:]], axis=0)
    out_ref[:, 2] = dot(together, tail).astype(bf16).reshape(peers, 8, HALF)


def combine_kernel(got_ref, rank_ref, weight_ref, mixer_ref, out_ref, total):
    block = pl.program_id(0)
    rows = got_ref.shape[0]
    tokens, experts = rank_ref.shape

    @pl.when(block == 0)
    def _():
        total[...] = jnp.zeros_like(total)

    member = expert_of(block, rows, experts)
    ranked = dot_last(rank_ref[...].astype(bf16), member)
    weight = dot_last(weight_ref[...].astype(bf16), member)
    slot, second = slots(iota((tokens, rows), 1, f32))
    weight = jnp.where(ranked == slot, weight, 0.0)
    first_half = jnp.where(second, 0.0, weight).astype(bf16)
    second_half = jnp.where(second, weight, 0.0).astype(bf16)
    total[...] += dot(jnp.concatenate([first_half, second_half], axis=0), got_ref[...])

    @pl.when(block == pl.num_programs(0) - 1)
    def _():
        out_ref[:, :HALF] = (mixer_ref[:, :HALF].astype(f32) + total[:tokens]).astype(bf16)
        out_ref[:, HALF:] = (mixer_ref[:, HALF:].astype(f32) + total[tokens:]).astype(bf16)


def fixed(*shape):
    return pl.BlockSpec(shape, lambda *_: (0,) * len(shape))


def fixed_once(*shape):
    return pl.BlockSpec(
        shape, lambda *_: (0,) * len(shape), pipeline_mode=pl.Buffered(1)
    )


def by_rows(*shape):
    rest = (0,) * (len(shape) - 1)
    return pl.BlockSpec(shape, lambda i, *_: (i, *rest))


def shape_of(kind, *shape):
    return jax.ShapeDtypeStruct(shape, kind)


def body(
    hidden,
    mixer_gain,
    gate_proj,
    value_proj,
    state_proj,
    log_decay,
    step_size,
    skip_gain,
    group_gain,
    out_proj,
    moe_gain,
    router,
    expert_ids,
    expert_gate_up,
    expert_down,
):
    rows = hidden.shape[0]
    heads = log_decay.shape[1]
    channels = heads * P_SIZE
    blocks = rows // Q
    seq_count = lax.axis_size("seq")
    exp_count = lax.axis_size("exp")
    peers = seq_count * exp_count
    place = lax.axis_index("exp")
    core, line = place % 2, place // 2
    lines = exp_count // 2
    own_rows = rows // exp_count
    slice_rows = N // seq_count

    swap = [(i, i ^ 1) for i in range(exp_count)]
    other_proj = lax.ppermute(out_proj, "exp", swap)

    mixed, x, maps, enter, sent = pl.pallas_call(
        local_state_kernel,
        grid=(blocks,),
        in_specs=[
            by_rows(Q, D),
            fixed(1, D),
            fixed_once(D, channels),
            fixed_once(D, 2 * N),
            by_rows(Q, heads),
            by_rows(Q, heads),
        ],
        out_specs=[
            by_rows(Q, D),
            by_rows(Q, channels),
            by_rows(Q, 2 * N),
            by_rows(1, N, channels),
            fixed(seq_count, slice_rows + 8, channels),
        ],
        out_shape=[
            shape_of(bf16, rows, D),
            shape_of(bf16, rows, channels),
            shape_of(bf16, rows, 2 * N),
            shape_of(bf16, blocks, N, channels),
            shape_of(bf16, seq_count, slice_rows + 8, channels),
        ],
        scratch_shapes=[pltpu.VMEM((N, channels), f32), pltpu.VMEM((8, heads), f32)],
        compiler_params=params(),
        cost_estimate=cost(2 * rows * D * (channels + 2 * N), 16 * 2**20),
        name="local_state",
    )(hidden, mixer_gain.reshape(1, D), value_proj, state_proj, log_decay, step_size)

    slices = lax.all_to_all(sent, "seq", split_axis=0, concat_axis=0, tiled=True)
    before = pl.pallas_call(
        prefix_kernel,
        out_shape=shape_of(bf16, seq_count, slice_rows, channels),
        compiler_params=pltpu.CompilerParams(vmem_limit_bytes=VMEM_LIMIT),
        name="prefix",
    )(slices)
    incoming = lax.all_to_all(before, "seq", split_axis=0, concat_axis=0, tiled=True)
    incoming = incoming.reshape(N, channels)

    gate, within = pl.pallas_call(
        within_kernel,
        grid=(blocks,),
        in_specs=[
            by_rows(Q, D),
            fixed_once(D, channels),
            by_rows(Q, channels),
            by_rows(Q, 2 * N),
            by_rows(Q, heads),
            by_rows(Q, heads),
        ],
        out_specs=[by_rows(Q, channels), by_rows(Q, channels)],
        out_shape=[shape_of(bf16, rows, channels), shape_of(f32, rows, channels)],
        compiler_params=params(),
        cost_estimate=cost(2 * rows * channels * (D + Q), 12 * 2**20, rows * Q * heads),
        name="within",
    )(mixed, gate_proj, x, maps, log_decay, step_size)

    own, other = pl.pallas_call(
        normed_kernel,
        grid_spec=pltpu.PrefetchScalarGridSpec(
            num_scalar_prefetch=1,
            grid=(blocks,),
            in_specs=[
                by_rows(Q, channels),
                by_rows(Q, channels),
                by_rows(Q, 2 * N),
                by_rows(Q, channels),
                by_rows(Q, heads),
                by_rows(1, N, channels),
                fixed(N, channels),
                fixed(1, heads),
                fixed(1, channels),
            ],
            out_specs=[by_rows(own_rows, channels), by_rows(own_rows, channels)],
            scratch_shapes=[pltpu.VMEM((8, heads), f32)],
        ),
        out_shape=[shape_of(bf16, rows // 2, channels)] * 2,
        compiler_params=params(),
        cost_estimate=cost(2 * rows * N * channels, 8 * 2**20),
        name="normed",
    )(
        core.reshape(1),
        within,
        x,
        maps,
        gate,
        log_decay,
        enter,
        incoming,
        skip_gain.reshape(1, heads),
        group_gain.reshape(1, channels),
    )
    got = lax.ppermute(other, "exp", swap)

    def project(target):
        return pl.pallas_call(
            project_kernel,
            grid_spec=pltpu.PrefetchScalarGridSpec(
                num_scalar_prefetch=1,
                grid=(1,),
                in_specs=[
                    pl.BlockSpec((own_rows, channels), lambda i, at: (at[0], 0)),
                    pl.BlockSpec((own_rows, channels), lambda i, at: (at[0], 0)),
                    fixed_once(channels, D),
                    fixed_once(channels, D),
                ],
                out_specs=fixed(own_rows, D),
            ),
            out_shape=shape_of(bf16, own_rows, D),
            compiler_params=params(),
            cost_estimate=cost(4 * own_rows * channels * D, 5 * 2**20),
            name="project",
        )(target.reshape(1), own, got, out_proj, other_proj)

    pieces = []
    for hop in (2, 1, 3):
        partial = project((line + hop) % lines)
        pieces.append(
            lax.ppermute(
                partial, "exp", [(i, (i + 2 * hop) % exp_count) for i in range(exp_count)]
            )
        )
    mine = project(line)

    experts = router.shape[1]
    slab_rows = experts * SLAB
    per_step = slab_rows // 4
    mixer_out, rank, weight, outgoing = pl.pallas_call(
        dispatch_kernel,
        grid_spec=pltpu.PrefetchScalarGridSpec(
            num_scalar_prefetch=1,
            grid=(4,),
            in_specs=[fixed(own_rows, D)] * 4
            + [
                pl.BlockSpec((own_rows, D), lambda i, at: (at[0], 0)),
                fixed(1, D),
                fixed(D, experts),
                fixed(own_rows, expert_ids.shape[1]),
            ],
            out_specs=[
                fixed(own_rows, D),
                fixed(own_rows, experts),
                fixed(own_rows, experts),
                by_rows(per_step, HALF),
            ],
            scratch_shapes=[
                pltpu.VMEM((2 * own_rows, HALF), bf16),
                pltpu.VMEM((own_rows, experts), bf16),
            ],
        ),
        out_shape=[
            shape_of(bf16, own_rows, D),
            shape_of(f32, own_rows, experts),
            shape_of(f32, own_rows, experts),
            shape_of(bf16, slab_rows, HALF),
        ],
        compiler_params=params(),
        cost_estimate=cost(4 * slab_rows * own_rows * HALF, 10 * 2**20),
        name="dispatch",
    )(
        place.reshape(1),
        mine,
        *pieces,
        hidden,
        moe_gain.reshape(1, D),
        router,
        expert_ids,
    )

    arrived = lax.all_to_all(
        outgoing.reshape(peers, SLAB, HALF),
        ("seq", "exp"),
        split_axis=0,
        concat_axis=0,
        tiled=True,
    ).reshape(peers, 3, 8, HALF)
    group = peers // 4

    def piece(index):
        return pl.BlockSpec((group, None, 8, HALF), lambda i: (i, index, 0, 0))

    results = pl.pallas_call(
        expert_kernel,
        grid=(4,),
        in_specs=[
            piece(0),
            piece(1),
            piece(2),
            fixed_once(1, D, 2 * F),
            fixed_once(1, F, D),
        ],
        out_specs=by_rows(group, 3, 8, HALF),
        out_shape=shape_of(bf16, peers, 3, 8, HALF),
        compiler_params=params(),
        cost_estimate=cost(6 * peers * CAP * D * F, 22 * 2**20, peers * CAP * F),
        name="experts",
    )(arrived, arrived, arrived, expert_gate_up, expert_down)
    returned = lax.all_to_all(
        results.reshape(peers, SLAB, HALF),
        ("seq", "exp"),
        split_axis=0,
        concat_axis=0,
        tiled=True,
    ).reshape(slab_rows, HALF)

    layer_out = pl.pallas_call(
        combine_kernel,
        grid=(4,),
        in_specs=[
            by_rows(per_step, HALF),
            fixed(own_rows, experts),
            fixed(own_rows, experts),
            fixed(own_rows, D),
        ],
        out_specs=fixed(own_rows, D),
        out_shape=shape_of(bf16, own_rows, D),
        scratch_shapes=[pltpu.VMEM((2 * own_rows, HALF), f32)],
        compiler_params=params(),
        cost_estimate=cost(4 * slab_rows * own_rows * HALF, 8 * 2**20),
        name="combine",
    )(returned, rank, weight, mixer_out)
    return (mixer_out, layer_out)


def solution(mesh):
    in_specs = (
        P("seq", None),
        P(),
        P(None, "exp"),
        P(None, "exp"),
        P(None, "exp"),
        P("seq", "exp"),
        P("seq", "exp"),
        P("exp"),
        P("exp"),
        P("exp", None),
        P(),
        P(),
        P(("seq", "exp"), None),
        P(("seq", "exp"), None, None),
        P(("seq", "exp"), None, None),
    )
    out_specs = (P(("seq", "exp"), None), P(("seq", "exp"), None))
    return jax.shard_map(body, mesh=mesh, in_specs=in_specs, out_specs=out_specs, check_vma=False)
```

```python
import jax
import jax.numpy as jnp
from jax import lax
from jax.experimental import pallas as pl
from jax.experimental.pallas import tpu as pltpu
from jax.sharding import PartitionSpec as P

D = 2048
HALF = D // 2
P_SIZE = 64
N = 128
Q = 256
F = 768
CAP = 12
SLAB = 2 * CAP

f32 = jnp.float32
bf16 = jnp.bfloat16
epsilon = 1e-05
LOG2_E = 1.4426950408889634


def params(mib):
    return pltpu.CompilerParams(
        dimension_semantics=("arbitrary",), vmem_limit_bytes=mib * 2**20
    )


def cost(flops, nbytes, transcendentals=0):
    return pl.CostEstimate(
        flops=int(flops), bytes_accessed=int(nbytes), transcendentals=int(transcendentals)
    )


def iota(shape, axis, kind=jnp.int32):
    return lax.broadcasted_iota(jnp.int32, shape, axis).astype(kind)


def dot(a, b):
    return jnp.dot(a, b, preferred_element_type=f32)


def dot_first(a, b):
    return lax.dot_general(a, b, (((0,), (0,)), ((), ())), preferred_element_type=f32)


def dot_last(a, b):
    return lax.dot_general(a, b, (((1,), (1,)), ((), ())), preferred_element_type=f32)


def running_sum(rates):
    heads, count = rates.shape
    upper = (iota((count, count), 0) <= iota((count, count), 1)).astype(f32).astype(bf16)
    terms = []
    for _ in range(3):
        term = rates.astype(bf16)
        terms.append(term)
        rates = rates - term.astype(f32)
    sums = dot(jnp.concatenate(terms, axis=0), upper)
    return sums[:heads] + (sums[heads : 2 * heads] + sums[2 * heads :])


def per_channel(values):
    heads = values.shape[0]
    lanes = heads * P_SIZE
    first = iota((heads, lanes), 0) * P_SIZE
    lane = iota((heads, lanes), 1)
    spread = ((lane >= first) & (lane < first + P_SIZE)).astype(f32)
    coarse = values.astype(bf16).astype(f32)
    terms = jnp.concatenate([coarse, values - coarse], axis=0).astype(bf16)
    return dot_first(terms, jnp.concatenate([spread, spread], axis=0).astype(bf16))


def row_per_channel(column):
    return per_channel(jnp.broadcast_to(column, (column.shape[0], 128)))[0:1]


def local_state_kernel(
    hidden_ref,
    gain_ref,
    value_ref,
    state_ref,
    decay_ref,
    step_ref,
    mixed_ref,
    x_ref,
    maps_ref,
    enter_ref,
    sent_ref,
    state,
    total,
):
    block = pl.program_id(0)

    @pl.when(block == 0)
    def _():
        state[...] = jnp.zeros_like(state)
        total[...] = jnp.zeros_like(total)

    wide = hidden_ref[...].astype(f32)
    scale = lax.rsqrt(jnp.mean(wide * wide, axis=-1, keepdims=True) + epsilon)
    mixed = (wide * scale * gain_ref[...]).astype(bf16)
    mixed_ref[...] = mixed
    x = dot(mixed, value_ref[...]).astype(bf16)
    x_ref[...] = x
    maps = dot(mixed, state_ref[...]).astype(bf16)
    maps_ref[...] = maps
    sums = running_sum(decay_ref[...])
    end = sums[:, Q - 1 : Q]
    weight = per_channel(jnp.exp(end - sums) * step_ref[...])
    weighted = (x.astype(f32) * weight).astype(bf16)
    old = state[...]
    enter_ref[0] = old.astype(bf16)
    new = old * row_per_channel(jnp.exp(end)) + dot_first(maps[:, :N], weighted)
    state[...] = new
    total[...] = total[...] + end

    @pl.when(block == pl.num_programs(0) - 1)
    def _():
        parts = sent_ref.shape[0]
        channels = new.shape[1]
        log_total = row_per_channel(total[:, 0:1])
        coarse = log_total.astype(bf16).astype(f32)
        which = iota((8, channels), 0)
        tail = jnp.where(which == 0, coarse, jnp.where(which == 1, log_total - coarse, 0.0))
        rows = new.reshape(parts, N // parts, channels)
        sent_ref[...] = jnp.concatenate(
            [rows, jnp.broadcast_to(tail[None], (parts, 8, channels))], axis=1
        ).astype(bf16)


def prefix_kernel(got_ref, out_ref):
    count = got_ref.shape[0]
    rows = out_ref.shape[1]
    carry = jnp.zeros(out_ref.shape[1:], f32)
    for shard in range(count):
        out_ref[shard] = carry.astype(bf16)
        got = got_ref[shard].astype(f32)
        decay = jnp.exp(got[rows : rows + 1] + got[rows + 1 : rows + 2])
        carry = decay * carry + got[:rows]


def gate_kernel(mixed_ref, gate_w_ref, gate_ref):
    gate_ref[...] = dot(mixed_ref[...], gate_w_ref[...]).astype(bf16)


def within_kernel(x_ref, maps_ref, decay_ref, step_ref, enter_ref, skip_ref, within_ref):
    sums = running_sum(decay_ref[...])
    heads = sums.shape[0]
    maps = maps_ref[...]
    part = Q // 2
    scores = dot_last(maps[:, N:], maps[:, :N])
    from_start = per_channel(jnp.exp(sums)) * dot(maps[:, N:], enter_ref[0])
    scaled = sums * LOG2_E
    source = scaled - jnp.log2(step_ref[...])
    blank = jnp.zeros((128 - heads, Q), f32)
    target = jnp.concatenate([scaled, blank], axis=0).T
    causal = iota((part, part), 0) >= iota((part, part), 1)
    left = (iota((Q, 2 * P_SIZE), 1) < P_SIZE).astype(f32).astype(bf16)
    right = (iota((Q, 2 * P_SIZE), 1) >= P_SIZE).astype(f32).astype(bf16)
    for pair in range(heads // 2):
        top, bottom = [], []
        for head in (2 * pair, 2 * pair + 1):
            column = target[:, head : head + 1]
            row = source[head : head + 1]
            corner = jnp.where(causal, column[:part] - row[:, :part], -jnp.inf)
            top.append((scores[:part, :part] * jnp.exp2(corner)).astype(bf16))
            past = column[part:] - row[:, :part]
            bottom.append((scores[part:, :part] * jnp.exp2(past)).astype(bf16))
            corner = jnp.where(causal, column[part:] - row[:, part:], -jnp.inf)
            bottom.append((scores[part:, part:] * jnp.exp2(corner)).astype(bf16))
        lanes = slice(pair * 2 * P_SIZE, (pair + 1) * 2 * P_SIZE)
        x = x_ref[:, lanes]
        x_left, x_right = x * left, x * right
        skip = x.astype(f32) * skip_ref[:, lanes] + from_start[:, lanes]
        within_ref[:part, lanes] = skip[:part] + dot(
            jnp.concatenate(top, axis=1),
            jnp.concatenate([x_left[:part], x_right[:part]], axis=0),
        )
        within_ref[part:, lanes] = skip[part:] + dot(
            jnp.concatenate(bottom, axis=1), jnp.concatenate([x_left, x_right], axis=0)
        )


def normed_kernel(
    core_ref,
    within_ref,
    maps_ref,
    gate_ref,
    decay_ref,
    incoming_ref,
    gain_ref,
    own_ref,
    other_ref,
    before,
):
    block = pl.program_id(0)

    @pl.when(block == 0)
    def _():
        before[...] = jnp.zeros_like(before)

    sums = running_sum(decay_ref[...]) + before[:, 0:1]
    before[...] = jnp.broadcast_to(sums[:, Q - 1 : Q], before.shape)
    carried = per_channel(jnp.exp(sums)) * dot(maps_ref[...], incoming_ref[...])
    gate = gate_ref[...].astype(f32)
    gated = (within_ref[...] + carried) * (gate * jax.nn.sigmoid(gate))
    scale = lax.rsqrt(jnp.mean(gated * gated, axis=-1, keepdims=True) + epsilon)
    normed = gated * scale * gain_ref[...]
    rows = own_ref.shape[0]
    first, second = normed[:rows], normed[rows:]
    mine = core_ref[0] == 0
    own_ref[...] = jnp.where(mine, first, second).astype(bf16)
    other_ref[...] = jnp.where(mine, second, first).astype(bf16)


def project_kernel(where_ref, own_ref, got_ref, own_w_ref, got_w_ref, out_ref):
    out_ref[...] = (
        dot(own_ref[...], own_w_ref[...]) + dot(got_ref[...], got_w_ref[...])
    ).astype(bf16)


def slots(row):
    place = row - SLAB * jnp.floor((row + 0.5) * (1.0 / SLAB))
    slot = jnp.where(place < 8, place, jnp.where(place < 20, place - 8, place - 12))
    second = ((place >= 8) & (place < 16)) | (place >= 20)
    return slot, second


def expert_of(block, rows, experts):
    gap = iota((rows, experts), 0) + block * rows - SLAB * iota((rows, experts), 1)
    return ((gap >= 0) & (gap < SLAB)).astype(f32).astype(bf16)


def route_kernel(ids_ref, named_ref, rank_ref, picker_ref, ranks):
    block = pl.program_id(0)
    tokens, experts = named_ref.shape

    @pl.when(block == 0)
    def _():
        lane = iota((tokens, experts), 1)
        named = jnp.zeros((tokens, experts), f32)
        for k in range(ids_ref.shape[1]):
            named = named + (ids_ref[:, k : k + 1] == lane).astype(f32)
        named_ref[...] = named
        earlier = (iota((tokens, tokens), 0) > iota((tokens, tokens), 1)).astype(f32)
        rank = dot(earlier.astype(bf16), named.astype(bf16))
        rank = jnp.where(named > 0.5, rank, -1.0)
        rank_ref[...] = rank
        ranks[...] = rank.astype(bf16)

    rows = picker_ref.shape[0]
    ranked = dot_last(expert_of(block, rows, experts), ranks[...])
    slot, second = slots(iota((rows, tokens), 0, f32))
    hit = (ranked == slot).astype(f32)
    picker_ref[:, :tokens] = jnp.where(second, 0.0, hit).astype(bf16)
    picker_ref[:, tokens:] = jnp.where(second, hit, 0.0).astype(bf16)


def dispatch_kernel(
    where_ref,
    a_ref,
    b_ref,
    c_ref,
    d_ref,
    hidden_ref,
    gain_ref,
    router_ref,
    named_ref,
    picker_ref,
    mixer_ref,
    weight_ref,
    out_ref,
    rows_in,
):
    block = pl.program_id(0)
    tokens = named_ref.shape[0]

    @pl.when(block == 0)
    def _():
        head_sum = (
            a_ref[...].astype(f32)
            + b_ref[...].astype(f32)
            + c_ref[...].astype(f32)
            + d_ref[...].astype(f32)
        )
        mixer_out = (hidden_ref[...].astype(f32) + head_sum).astype(bf16)
        mixer_ref[...] = mixer_out
        wide = mixer_out.astype(f32)
        scale = lax.rsqrt(jnp.mean(wide * wide, axis=-1, keepdims=True) + epsilon)
        expert_input = (wide * scale * gain_ref[...]).astype(bf16)
        rows_in[:tokens, :] = expert_input[:, :HALF]
        rows_in[tokens:, :] = expert_input[:, HALF:]
        picked = named_ref[...] * jax.nn.sigmoid(dot(expert_input, router_ref[...]))
        weight_ref[...] = picked / jnp.sum(picked, axis=-1, keepdims=True)

    out_ref[...] = dot(picker_ref[...], rows_in[...]).astype(bf16)


def expert_kernel(a_ref, b_ref, c_ref, up_ref, down_ref, out_ref):
    peers = a_ref.shape[0]
    rows = peers * 8
    part = rows // 2
    place = iota((rows, rows), 0)
    lane = iota((rows, rows), 1)

    def source(row):
        inner = row & (part - 1)
        return ((inner >> 2) << 3) + jnp.where(row >= part, 4, 0) + (inner & 3)

    apart = (source(place) == lane).astype(f32).astype(bf16)
    together = (place == source(lane)).astype(f32).astype(bf16)
    tail = dot(apart, c_ref[...].reshape(rows, HALF)).astype(bf16)
    x0 = jnp.concatenate([a_ref[...].reshape(rows, HALF), tail[:part]], axis=0)
    x1 = jnp.concatenate([b_ref[...].reshape(rows, HALF), tail[part:]], axis=0)
    projected = dot(x0, up_ref[0, :HALF]) + dot(x1, up_ref[0, HALF:])
    gate = projected[:, :F]
    hidden = (gate * jax.nn.sigmoid(gate) * projected[:, F:]).astype(bf16)
    y0 = dot(hidden, down_ref[0, :, :HALF]).astype(bf16)
    y1 = dot(hidden, down_ref[0, :, HALF:]).astype(bf16)
    out_ref[:, 0] = y0[:rows].reshape(peers, 8, HALF)
    out_ref[:, 1] = y1[:rows].reshape(peers, 8, HALF)
    tail = jnp.concatenate([y0[rows:], y1[rows:]], axis=0)
    out_ref[:, 2] = dot(together, tail).astype(bf16).reshape(peers, 8, HALF)


def combine_weight_kernel(rank_ref, weight_ref, out_ref):
    block = pl.program_id(0)
    tokens, experts = rank_ref.shape
    rows = out_ref.shape[1]
    member = expert_of(block, rows, experts)
    ranked = dot_last(rank_ref[...].astype(bf16), member)
    weight = dot_last(weight_ref[...].astype(bf16), member)
    slot, second = slots(iota((tokens, rows), 1, f32))
    weight = jnp.where(ranked == slot, weight, 0.0)
    out_ref[:tokens] = jnp.where(second, 0.0, weight).astype(bf16)
    out_ref[tokens:] = jnp.where(second, weight, 0.0).astype(bf16)


def combine_kernel(got_ref, weight_ref, mixer_ref, out_ref, total):
    block = pl.program_id(0)
    tokens = mixer_ref.shape[0]

    @pl.when(block == 0)
    def _():
        total[...] = jnp.zeros_like(total)

    total[...] += dot(weight_ref[...], got_ref[...])

    @pl.when(block == pl.num_programs(0) - 1)
    def _():
        out_ref[:, :HALF] = (mixer_ref[:, :HALF].astype(f32) + total[:tokens]).astype(bf16)
        out_ref[:, HALF:] = (mixer_ref[:, HALF:].astype(f32) + total[tokens:]).astype(bf16)


def fixed(*shape):
    return pl.BlockSpec(shape, lambda *_: (0,) * len(shape))


def fixed_once(*shape):
    return pl.BlockSpec(
        shape, lambda *_: (0,) * len(shape), pipeline_mode=pl.Buffered(1)
    )


def by_rows(*shape):
    rest = (0,) * (len(shape) - 1)
    return pl.BlockSpec(shape, lambda i, *_: (i, *rest))


def by_lanes(*shape):
    return pl.BlockSpec(shape, lambda i, *_: (0, i))


def resident():
    return pl.BlockSpec(memory_space=pltpu.VMEM)


def shape_of(kind, *shape):
    return jax.ShapeDtypeStruct(shape, kind)


def stored(kind, *shape):
    return pltpu.HBM(shape, kind)


def from_hbm(*arrays):
    return [pltpu.with_memory_space_constraint(a, pltpu.HBM) for a in arrays]


def from_vmem(*arrays):
    return [pltpu.with_memory_space_constraint(a, pltpu.VMEM) for a in arrays]


def body(
    hidden,
    mixer_gain,
    gate_proj,
    value_proj,
    state_proj,
    log_decay,
    step_size,
    skip_gain,
    group_gain,
    out_proj,
    moe_gain,
    router,
    expert_ids,
    expert_gate_up,
    expert_down,
):
    rows = hidden.shape[0]
    heads = log_decay.shape[1]
    channels = heads * P_SIZE
    blocks = rows // Q
    seq_count = lax.axis_size("seq")
    exp_count = lax.axis_size("exp")
    peers = seq_count * exp_count
    place = lax.axis_index("exp")
    core, line = place % 2, place // 2
    lines = exp_count // 2
    own_rows = rows // exp_count
    slice_rows = N // seq_count
    experts = router.shape[1]
    slab_rows = experts * SLAB
    per_step = slab_rows // 4

    swap = [(i, i ^ 1) for i in range(exp_count)]
    other_proj = lax.ppermute(out_proj, "exp", swap)
    decay = log_decay.T
    step = step_size.T

    mixed, x, maps, enter, sent = pl.pallas_call(
        local_state_kernel,
        grid=(blocks,),
        in_specs=[
            by_rows(Q, D),
            fixed(1, D),
            fixed_once(D, channels),
            fixed_once(D, 2 * N),
            by_lanes(heads, Q),
            by_lanes(heads, Q),
        ],
        out_specs=[
            by_rows(Q, D),
            by_rows(Q, channels),
            by_rows(Q, 2 * N),
            by_rows(1, N, channels),
            fixed(seq_count, slice_rows + 8, channels),
        ],
        out_shape=[
            stored(bf16, rows, D),
            stored(bf16, rows, channels),
            stored(bf16, rows, 2 * N),
            stored(bf16, blocks, N, channels),
            shape_of(bf16, seq_count, slice_rows + 8, channels),
        ],
        scratch_shapes=[pltpu.VMEM((N, channels), f32), pltpu.VMEM((heads, 128), f32)],
        compiler_params=params(24),
        cost_estimate=cost(2 * rows * D * (channels + 2 * N), 16 * 2**20),
        name="local_state",
    )(*from_hbm(hidden, mixer_gain.reshape(1, D), value_proj, state_proj, decay, step))

    slices = lax.all_to_all(sent, "seq", split_axis=0, concat_axis=0, tiled=True)

    gate = pl.pallas_call(
        gate_kernel,
        grid=(blocks,),
        in_specs=[by_rows(Q, D), fixed_once(D, channels)],
        out_specs=by_rows(Q, channels),
        out_shape=stored(bf16, rows, channels),
        compiler_params=params(12),
        cost_estimate=cost(2 * rows * channels * D, 7 * 2**20),
        name="gate",
    )(*from_hbm(mixed, gate_proj))
    named, rank, picker = pl.pallas_call(
        route_kernel,
        grid=(4,),
        in_specs=[fixed(own_rows, expert_ids.shape[1])],
        out_specs=[
            fixed(own_rows, experts),
            fixed(own_rows, experts),
            by_rows(per_step, 2 * own_rows),
        ],
        out_shape=[
            shape_of(f32, own_rows, experts),
            shape_of(f32, own_rows, experts),
            stored(bf16, slab_rows, 2 * own_rows),
        ],
        scratch_shapes=[pltpu.VMEM((own_rows, experts), bf16)],
        compiler_params=params(12),
        cost_estimate=cost(2 * slab_rows * experts * own_rows, 4 * 2**20),
        name="route",
    )(expert_ids)
    slices, gate, named, rank, picker = lax.optimization_barrier(
        (slices, gate, named, rank, picker)
    )

    before = pl.pallas_call(
        prefix_kernel,
        out_shape=shape_of(bf16, seq_count, slice_rows, channels),
        compiler_params=pltpu.CompilerParams(vmem_limit_bytes=8 * 2**20),
        name="prefix",
    )(slices)
    incoming = lax.all_to_all(before, "seq", split_axis=0, concat_axis=0, tiled=True)
    incoming = incoming.reshape(N, channels)

    within = pl.pallas_call(
        within_kernel,
        grid=(blocks,),
        in_specs=[
            by_rows(Q, channels),
            by_rows(Q, 2 * N),
            by_lanes(heads, Q),
            by_lanes(heads, Q),
            by_rows(1, N, channels),
            fixed(1, channels),
        ],
        out_specs=by_rows(Q, channels),
        out_shape=stored(f32, rows, channels),
        compiler_params=params(16),
        cost_estimate=cost(4 * rows * channels * Q, 6 * 2**20, rows * Q * heads),
        name="within",
    )(
        *from_hbm(x, maps, decay, step, enter),
        jnp.repeat(skip_gain, P_SIZE).reshape(1, channels),
    )

    own, other = pl.pallas_call(
        normed_kernel,
        grid_spec=pltpu.PrefetchScalarGridSpec(
            num_scalar_prefetch=1,
            grid=(blocks,),
            in_specs=[
                by_rows(Q, channels),
                pl.BlockSpec((Q, N), lambda i, *_: (i, 1)),
                by_rows(Q, channels),
                by_lanes(heads, Q),
                fixed(N, channels),
                fixed(1, channels),
            ],
            out_specs=[by_rows(own_rows, channels), by_rows(own_rows, channels)],
            scratch_shapes=[pltpu.VMEM((heads, 128), f32)],
        ),
        out_shape=[shape_of(bf16, rows // 2, channels)] * 2,
        compiler_params=params(12),
        cost_estimate=cost(2 * rows * N * channels, 5 * 2**20),
        name="normed",
    )(
        core.reshape(1),
        *from_hbm(within, maps, gate, decay),
        incoming,
        group_gain.reshape(1, channels),
    )
    got = lax.ppermute(other, "exp", swap)

    projections = from_vmem(out_proj, other_proj)

    def project(target):
        return pl.pallas_call(
            project_kernel,
            grid_spec=pltpu.PrefetchScalarGridSpec(
                num_scalar_prefetch=1,
                grid=(1,),
                in_specs=[
                    pl.BlockSpec((own_rows, channels), lambda i, at: (at[0], 0)),
                    pl.BlockSpec((own_rows, channels), lambda i, at: (at[0], 0)),
                    resident(),
                    resident(),
                ],
                out_specs=fixed(own_rows, D),
            ),
            out_shape=shape_of(bf16, own_rows, D),
            compiler_params=params(8),
            cost_estimate=cost(4 * own_rows * channels * D, 5 * 2**20),
            name="project",
        )(target.reshape(1), own, got, *projections)

    pieces = []
    for hop in (2, 1, 3):
        partial = project((line + hop) % lines)
        pieces.append(
            lax.ppermute(
                partial, "exp", [(i, (i + 2 * hop) % exp_count) for i in range(exp_count)]
            )
        )
    mine = project(line)

    mixer_out, weight, outgoing = pl.pallas_call(
        dispatch_kernel,
        grid_spec=pltpu.PrefetchScalarGridSpec(
            num_scalar_prefetch=1,
            grid=(4,),
            in_specs=[fixed(own_rows, D)] * 4
            + [
                pl.BlockSpec((own_rows, D), lambda i, at: (at[0], 0)),
                fixed(1, D),
                fixed(D, experts),
                fixed(own_rows, experts),
                by_rows(per_step, 2 * own_rows),
            ],
            out_specs=[
                fixed(own_rows, D),
                fixed(own_rows, experts),
                by_rows(per_step, HALF),
            ],
            scratch_shapes=[pltpu.VMEM((2 * own_rows, HALF), bf16)],
        ),
        out_shape=[
            shape_of(bf16, own_rows, D),
            shape_of(f32, own_rows, experts),
            shape_of(bf16, slab_rows, HALF),
        ],
        compiler_params=params(24),
        cost_estimate=cost(4 * slab_rows * own_rows * HALF, 10 * 2**20),
        name="dispatch",
    )(
        place.reshape(1),
        mine,
        *pieces,
        *from_hbm(hidden, moe_gain.reshape(1, D), router),
        named,
        *from_hbm(picker),
    )

    arrived = lax.all_to_all(
        outgoing.reshape(peers, SLAB, HALF),
        ("seq", "exp"),
        split_axis=0,
        concat_axis=0,
        tiled=True,
    ).reshape(peers, 3, 8, HALF)
    group = peers // 4
    combine_weight = pl.pallas_call(
        combine_weight_kernel,
        grid=(4,),
        in_specs=[fixed(own_rows, experts), fixed(own_rows, experts)],
        out_specs=by_lanes(2 * own_rows, per_step),
        out_shape=stored(bf16, 2 * own_rows, slab_rows),
        compiler_params=params(12),
        cost_estimate=cost(4 * slab_rows * experts * own_rows, 4 * 2**20),
        name="combine_weight",
    )(rank, weight)

    def piece(index):
        return pl.BlockSpec((group, None, 8, HALF), lambda i: (i, index, 0, 0))

    results = pl.pallas_call(
        expert_kernel,
        grid=(4,),
        in_specs=[piece(0), piece(1), piece(2), resident(), resident()],
        out_specs=by_rows(group, 3, 8, HALF),
        out_shape=stored(bf16, peers, 3, 8, HALF),
        compiler_params=params(28),
        cost_estimate=cost(6 * peers * CAP * D * F, 22 * 2**20, peers * CAP * F),
        name="experts",
    )(arrived, arrived, arrived, *from_vmem(expert_gate_up, expert_down))
    returned = lax.all_to_all(
        results.reshape(peers, SLAB, HALF),
        ("seq", "exp"),
        split_axis=0,
        concat_axis=0,
        tiled=True,
    ).reshape(slab_rows, HALF)

    layer_out = pl.pallas_call(
        combine_kernel,
        grid=(4,),
        in_specs=[
            by_rows(per_step, HALF),
            by_lanes(2 * own_rows, per_step),
            fixed(own_rows, D),
        ],
        out_specs=fixed(own_rows, D),
        out_shape=shape_of(bf16, own_rows, D),
        scratch_shapes=[pltpu.VMEM((2 * own_rows, HALF), f32)],
        compiler_params=params(16),
        cost_estimate=cost(4 * slab_rows * own_rows * HALF, 8 * 2**20),
        name="combine",
    )(*from_hbm(returned, combine_weight, mixer_out))
    return (mixer_out, layer_out)


def solution(mesh):
    in_specs = (
        P("seq", None),
        P(),
        P(None, "exp"),
        P(None, "exp"),
        P(None, "exp"),
        P("seq", "exp"),
        P("seq", "exp"),
        P("exp"),
        P("exp"),
        P("exp", None),
        P(),
        P(),
        P(("seq", "exp"), None),
        P(("seq", "exp"), None, None),
        P(("seq", "exp"), None, None),
    )
    out_specs = (P(("seq", "exp"), None), P(("seq", "exp"), None))
    return jax.shard_map(body, mesh=mesh, in_specs=in_specs, out_specs=out_specs, check_vma=False)
```

```python
import jax
import jax.numpy as jnp
from jax import lax
from jax.experimental import pallas as pl
from jax.experimental.pallas import tpu as pltpu
from jax.sharding import PartitionSpec as P

D = 2048
HALF = D // 2
P_SIZE = 64
N = 128
Q = 256
F = 768
CAP = 12
SLAB = 2 * CAP

f32 = jnp.float32
bf16 = jnp.bfloat16
epsilon = 1e-05
LOG2_E = 1.4426950408889634


def params(mib):
    return pltpu.CompilerParams(
        dimension_semantics=("arbitrary",), vmem_limit_bytes=mib * 2**20
    )


def cost(flops, nbytes, transcendentals=0):
    return pl.CostEstimate(
        flops=int(flops), bytes_accessed=int(nbytes), transcendentals=int(transcendentals)
    )


def iota(shape, axis, kind=jnp.int32):
    return lax.broadcasted_iota(jnp.int32, shape, axis).astype(kind)


def dot(a, b):
    return jnp.dot(a, b, preferred_element_type=f32)


def dot_first(a, b):
    return lax.dot_general(a, b, (((0,), (0,)), ((), ())), preferred_element_type=f32)


def dot_last(a, b):
    return lax.dot_general(a, b, (((1,), (1,)), ((), ())), preferred_element_type=f32)


def running_sum(rates):
    heads, count = rates.shape
    upper = (iota((count, count), 0) <= iota((count, count), 1)).astype(f32).astype(bf16)
    terms = []
    for _ in range(3):
        term = rates.astype(bf16)
        terms.append(term)
        rates = rates - term.astype(f32)
    sums = dot(jnp.concatenate(terms, axis=0), upper)
    return sums[:heads] + (sums[heads : 2 * heads] + sums[2 * heads :])


def per_channel(values):
    heads = values.shape[0]
    lanes = heads * P_SIZE
    first = iota((heads, lanes), 0) * P_SIZE
    lane = iota((heads, lanes), 1)
    spread = ((lane >= first) & (lane < first + P_SIZE)).astype(f32)
    coarse = values.astype(bf16).astype(f32)
    terms = jnp.concatenate([coarse, values - coarse], axis=0).astype(bf16)
    return dot_first(terms, jnp.concatenate([spread, spread], axis=0).astype(bf16))


def row_per_channel(column):
    return per_channel(jnp.broadcast_to(column, (column.shape[0], 128)))[0:1]


def local_state_kernel(
    hidden_ref,
    gain_ref,
    value_ref,
    state_ref,
    decay_ref,
    step_ref,
    mixed_ref,
    x_ref,
    maps_ref,
    enter_ref,
    sent_ref,
    state,
    total,
):
    block = pl.program_id(0)

    @pl.when(block == 0)
    def _():
        state[...] = jnp.zeros_like(state)
        total[...] = jnp.zeros_like(total)

    wide = hidden_ref[...].astype(f32)
    scale = lax.rsqrt(jnp.mean(wide * wide, axis=-1, keepdims=True) + epsilon)
    mixed = (wide * scale * gain_ref[...]).astype(bf16)
    mixed_ref[...] = mixed
    x = dot(mixed, value_ref[...]).astype(bf16)
    x_ref[...] = x
    maps = dot(mixed, state_ref[...]).astype(bf16)
    maps_ref[...] = maps
    sums = running_sum(decay_ref[...])
    end = sums[:, Q - 1 : Q]
    weight = per_channel(jnp.exp(end - sums) * step_ref[...])
    weighted = (x.astype(f32) * weight).astype(bf16)
    old = state[...]
    enter_ref[0] = old.astype(bf16)
    new = old * row_per_channel(jnp.exp(end)) + dot_first(maps[:, :N], weighted)
    state[...] = new
    total[...] = total[...] + end

    @pl.when(block == pl.num_programs(0) - 1)
    def _():
        parts = sent_ref.shape[0]
        channels = new.shape[1]
        log_total = row_per_channel(total[:, 0:1])
        coarse = log_total.astype(bf16).astype(f32)
        which = iota((8, channels), 0)
        tail = jnp.where(which == 0, coarse, jnp.where(which == 1, log_total - coarse, 0.0))
        rows = new.reshape(parts, N // parts, channels)
        sent_ref[...] = jnp.concatenate(
            [rows, jnp.broadcast_to(tail[None], (parts, 8, channels))], axis=1
        ).astype(bf16)


def prefix_kernel(got_ref, out_ref):
    count = got_ref.shape[0]
    rows = out_ref.shape[1]
    carry = jnp.zeros(out_ref.shape[1:], f32)
    for shard in range(count):
        out_ref[shard] = carry.astype(bf16)
        got = got_ref[shard].astype(f32)
        decay = jnp.exp(got[rows : rows + 1] + got[rows + 1 : rows + 2])
        carry = decay * carry + got[:rows]


def gate_kernel(mixed_ref, gate_w_ref, gate_ref):
    gate_ref[...] = dot(mixed_ref[...], gate_w_ref[...]).astype(bf16)


def within_kernel(x_ref, maps_ref, decay_ref, step_ref, enter_ref, skip_ref, within_ref):
    sums = running_sum(decay_ref[...])
    heads = sums.shape[0]
    maps = maps_ref[...]
    part = Q // 2
    scores = dot_last(maps[:, N:], maps[:, :N])
    from_start = per_channel(jnp.exp(sums)) * dot(maps[:, N:], enter_ref[0])
    scaled = sums * LOG2_E
    source = scaled - jnp.log2(step_ref[...])
    blank = jnp.zeros((128 - heads, Q), f32)
    target = jnp.concatenate([scaled, blank], axis=0).T
    causal = iota((part, part), 0) >= iota((part, part), 1)
    left = (iota((Q, 2 * P_SIZE), 1) < P_SIZE).astype(f32).astype(bf16)
    right = (iota((Q, 2 * P_SIZE), 1) >= P_SIZE).astype(f32).astype(bf16)
    for pair in range(heads // 2):
        top, bottom = [], []
        for head in (2 * pair, 2 * pair + 1):
            column = target[:, head : head + 1]
            row = source[head : head + 1]
            corner = jnp.where(causal, column[:part] - row[:, :part], -jnp.inf)
            top.append((scores[:part, :part] * jnp.exp2(corner)).astype(bf16))
            past = column[part:] - row[:, :part]
            bottom.append((scores[part:, :part] * jnp.exp2(past)).astype(bf16))
            corner = jnp.where(causal, column[part:] - row[:, part:], -jnp.inf)
            bottom.append((scores[part:, part:] * jnp.exp2(corner)).astype(bf16))
        lanes = slice(pair * 2 * P_SIZE, (pair + 1) * 2 * P_SIZE)
        x = x_ref[:, lanes]
        x_left, x_right = x * left, x * right
        skip = x.astype(f32) * skip_ref[:, lanes] + from_start[:, lanes]
        within_ref[:part, lanes] = skip[:part] + dot(
            jnp.concatenate(top, axis=1),
            jnp.concatenate([x_left[:part], x_right[:part]], axis=0),
        )
        within_ref[part:, lanes] = skip[part:] + dot(
            jnp.concatenate(bottom, axis=1), jnp.concatenate([x_left, x_right], axis=0)
        )


def normed_kernel(
    core_ref,
    within_ref,
    maps_ref,
    gate_ref,
    decay_ref,
    incoming_ref,
    gain_ref,
    own_ref,
    other_ref,
    before,
):
    block = pl.program_id(0)

    @pl.when(block == 0)
    def _():
        before[...] = jnp.zeros_like(before)

    sums = running_sum(decay_ref[...]) + before[:, 0:1]
    before[...] = jnp.broadcast_to(sums[:, Q - 1 : Q], before.shape)
    carried = per_channel(jnp.exp(sums)) * dot(maps_ref[...], incoming_ref[...])
    gate = gate_ref[...].astype(f32)
    gated = (within_ref[...] + carried) * (gate * jax.nn.sigmoid(gate))
    scale = lax.rsqrt(jnp.mean(gated * gated, axis=-1, keepdims=True) + epsilon)
    normed = gated * scale * gain_ref[...]
    rows = own_ref.shape[0]
    first, second = normed[:rows], normed[rows:]
    mine = core_ref[0] == 0
    own_ref[...] = jnp.where(mine, first, second).astype(bf16)
    other_ref[...] = jnp.where(mine, second, first).astype(bf16)


def own_part_kernel(at_ref, own_ref, own_w_ref, got_w_ref, part_ref, kept_ref):
    part_ref[...] = dot(own_ref[...], own_w_ref[...])
    kept_ref[...] = got_w_ref[...]


def finish_kernel(at_ref, part_ref, got_ref, got_w_ref, left_ref, right_ref):
    out = part_ref[...] + dot(got_ref[...], got_w_ref[...])
    left_ref[...] = out[:, :HALF].astype(bf16)
    right_ref[...] = out[:, HALF:].astype(bf16)


def halves_kernel(
    at_ref, own_a_ref, got_a_ref, own_b_ref, got_b_ref, own_w_ref, got_w_ref, *rest
):
    *more, a_ref, b_ref = rest
    halves = (slice(0, HALF), slice(HALF, D))
    if not more:
        halves = halves[::-1]
    a = dot(own_a_ref[...], own_w_ref[:, halves[0]]) + dot(got_a_ref[...], got_w_ref[:, halves[0]])
    b = dot(own_b_ref[...], own_w_ref[:, halves[1]]) + dot(got_b_ref[...], got_w_ref[:, halves[1]])
    if more:
        a = a + more[0][...].astype(f32)
        b = b + more[1][...].astype(f32)
    a_ref[...] = a.astype(bf16)
    b_ref[...] = b.astype(bf16)


def slots(row):
    place = row - SLAB * jnp.floor((row + 0.5) * (1.0 / SLAB))
    slot = jnp.where(place < 8, place, jnp.where(place < 20, place - 8, place - 12))
    second = ((place >= 8) & (place < 16)) | (place >= 20)
    return slot, second


def expert_of(block, rows, experts):
    gap = iota((rows, experts), 0) + block * rows - SLAB * iota((rows, experts), 1)
    return ((gap >= 0) & (gap < SLAB)).astype(f32).astype(bf16)


def route_kernel(ids_ref, named_ref, rank_ref, picker_ref, ranks):
    block = pl.program_id(0)
    tokens, experts = named_ref.shape

    @pl.when(block == 0)
    def _():
        lane = iota((tokens, experts), 1)
        named = jnp.zeros((tokens, experts), f32)
        for k in range(ids_ref.shape[1]):
            named = named + (ids_ref[:, k : k + 1] == lane).astype(f32)
        named_ref[...] = named
        earlier = (iota((tokens, tokens), 0) > iota((tokens, tokens), 1)).astype(f32)
        rank = dot(earlier.astype(bf16), named.astype(bf16))
        rank = jnp.where(named > 0.5, rank, -1.0)
        rank_ref[...] = rank
        ranks[...] = rank.astype(bf16)

    rows = picker_ref.shape[0]
    ranked = dot_last(expert_of(block, rows, experts), ranks[...])
    slot, second = slots(iota((rows, tokens), 0, f32))
    hit = (ranked == slot).astype(f32)
    picker_ref[:, :tokens] = jnp.where(second, 0.0, hit).astype(bf16)
    picker_ref[:, tokens:] = jnp.where(second, hit, 0.0).astype(bf16)


def dispatch_kernel(
    where_ref,
    left_a_ref,
    left_b_ref,
    left_c_ref,
    right_a_ref,
    right_b_ref,
    right_c_ref,
    hidden_ref,
    gain_ref,
    router_ref,
    named_ref,
    picker_ref,
    mixer_ref,
    weight_ref,
    out_ref,
):
    left = left_a_ref[...].astype(f32) + left_b_ref[...].astype(f32)
    right = right_a_ref[...].astype(f32) + right_b_ref[...].astype(f32)
    head_sum = jnp.concatenate(
        [left + left_c_ref[...].astype(f32), right + right_c_ref[...].astype(f32)], axis=1
    )
    mixer_out = (hidden_ref[...].astype(f32) + head_sum).astype(bf16)
    mixer_ref[...] = mixer_out
    wide = mixer_out.astype(f32)
    scale = lax.rsqrt(jnp.mean(wide * wide, axis=-1, keepdims=True) + epsilon)
    expert_input = (wide * scale * gain_ref[...]).astype(bf16)
    rows_in = jnp.concatenate([expert_input[:, :HALF], expert_input[:, HALF:]], axis=0)
    picked = named_ref[...] * jax.nn.sigmoid(dot(expert_input, router_ref[...]))
    weight_ref[...] = picked / jnp.sum(picked, axis=-1, keepdims=True)
    step = out_ref.shape[0] // 8
    for i in range(8):
        part = slice(i * step, (i + 1) * step)
        out_ref[part] = dot(picker_ref[part], rows_in).astype(bf16)


def expert_kernel(a_ref, b_ref, c_ref, up_ref, down_ref, out_ref):
    peers = a_ref.shape[0]
    rows = peers * 8
    part = rows // 2
    place = iota((rows, rows), 0)
    lane = iota((rows, rows), 1)

    def source(row):
        inner = row & (part - 1)
        return ((inner >> 2) << 3) + jnp.where(row >= part, 4, 0) + (inner & 3)

    apart = (source(place) == lane).astype(f32).astype(bf16)
    together = (place == source(lane)).astype(f32).astype(bf16)
    tail = dot(apart, c_ref[...].reshape(rows, HALF)).astype(bf16)
    x0 = jnp.concatenate([a_ref[...].reshape(rows, HALF), tail[:part]], axis=0)
    x1 = jnp.concatenate([b_ref[...].reshape(rows, HALF), tail[part:]], axis=0)
    projected = dot(x0, up_ref[0, :HALF]) + dot(x1, up_ref[0, HALF:])
    gate = projected[:, :F]
    hidden = (gate * jax.nn.sigmoid(gate) * projected[:, F:]).astype(bf16)
    y0 = dot(hidden, down_ref[0, :, :HALF]).astype(bf16)
    y1 = dot(hidden, down_ref[0, :, HALF:]).astype(bf16)
    out_ref[:, 0] = y0[:rows].reshape(peers, 8, HALF)
    out_ref[:, 1] = y1[:rows].reshape(peers, 8, HALF)
    tail = jnp.concatenate([y0[rows:], y1[rows:]], axis=0)
    out_ref[:, 2] = dot(together, tail).astype(bf16).reshape(peers, 8, HALF)


def combine_weight_kernel(rank_ref, weight_ref, out_ref):
    block = pl.program_id(0)
    tokens, experts = rank_ref.shape
    rows = out_ref.shape[1]
    member = expert_of(block, rows, experts)
    ranked = dot_last(rank_ref[...].astype(bf16), member)
    weight = dot_last(weight_ref[...].astype(bf16), member)
    slot, second = slots(iota((tokens, rows), 1, f32))
    weight = jnp.where(ranked == slot, weight, 0.0)
    out_ref[:tokens] = jnp.where(second, 0.0, weight).astype(bf16)
    out_ref[tokens:] = jnp.where(second, weight, 0.0).astype(bf16)


def combine_kernel(got_ref, weight_ref, mixer_ref, out_ref, held, ready):
    tokens = mixer_ref.shape[0]
    parts, group = held.shape[0], held.shape[1]
    rows = group * SLAB

    def fetch(i):
        return pltpu.make_async_copy(
            got_ref.at[pl.ds(i * group, group)], held.at[i], ready.at[i]
        )

    for i in range(parts):
        fetch(i).start()
    total = jnp.zeros((2 * tokens, HALF), f32)
    for i in range(parts):
        fetch(i).wait()
        total += dot(weight_ref[:, i * rows : (i + 1) * rows], held[i].reshape(rows, HALF))
    out_ref[:, :HALF] = (mixer_ref[:, :HALF].astype(f32) + total[:tokens]).astype(bf16)
    out_ref[:, HALF:] = (mixer_ref[:, HALF:].astype(f32) + total[tokens:]).astype(bf16)


def fixed(*shape):
    return pl.BlockSpec(shape, lambda *_: (0,) * len(shape))


def fixed_once(*shape):
    return pl.BlockSpec(
        shape, lambda *_: (0,) * len(shape), pipeline_mode=pl.Buffered(1)
    )


def by_rows(*shape):
    rest = (0,) * (len(shape) - 1)
    return pl.BlockSpec(shape, lambda i, *_: (i, *rest))


def by_lanes(*shape):
    return pl.BlockSpec(shape, lambda i, *_: (0, i))


def resident():
    return pl.BlockSpec(memory_space=pltpu.VMEM)


def shape_of(kind, *shape):
    return jax.ShapeDtypeStruct(shape, kind)


def stored(kind, *shape):
    return pltpu.HBM(shape, kind)


def from_hbm(*arrays):
    return [pltpu.with_memory_space_constraint(a, pltpu.HBM) for a in arrays]


def from_vmem(*arrays):
    return [pltpu.with_memory_space_constraint(a, pltpu.VMEM) for a in arrays]


def body(
    hidden,
    mixer_gain,
    gate_proj,
    value_proj,
    state_proj,
    log_decay,
    step_size,
    skip_gain,
    group_gain,
    out_proj,
    moe_gain,
    router,
    expert_ids,
    expert_gate_up,
    expert_down,
):
    rows = hidden.shape[0]
    heads = log_decay.shape[1]
    channels = heads * P_SIZE
    blocks = rows // Q
    seq_count = lax.axis_size("seq")
    exp_count = lax.axis_size("exp")
    peers = seq_count * exp_count
    place = lax.axis_index("exp")
    core, line = place % 2, place // 2
    lines = exp_count // 2
    own_rows = rows // exp_count
    slice_rows = N // seq_count
    experts = router.shape[1]
    slab_rows = experts * SLAB
    per_step = slab_rows // 4

    swap = [(i, i ^ 1) for i in range(exp_count)]
    other_proj = lax.ppermute(out_proj, "exp", swap)
    decay = log_decay.T
    step = step_size.T

    mixed, x, maps, enter, sent = pl.pallas_call(
        local_state_kernel,
        grid=(blocks,),
        in_specs=[
            by_rows(Q, D),
            fixed(1, D),
            fixed_once(D, channels),
            fixed_once(D, 2 * N),
            by_lanes(heads, Q),
            by_lanes(heads, Q),
        ],
        out_specs=[
            by_rows(Q, D),
            by_rows(Q, channels),
            by_rows(Q, 2 * N),
            by_rows(1, N, channels),
            fixed(seq_count, slice_rows + 8, channels),
        ],
        out_shape=[
            stored(bf16, rows, D),
            stored(bf16, rows, channels),
            stored(bf16, rows, 2 * N),
            stored(bf16, blocks, N, channels),
            shape_of(bf16, seq_count, slice_rows + 8, channels),
        ],
        scratch_shapes=[pltpu.VMEM((N, channels), f32), pltpu.VMEM((heads, 128), f32)],
        compiler_params=params(24),
        cost_estimate=cost(2 * rows * D * (channels + 2 * N), 16 * 2**20),
        name="local_state",
    )(*from_hbm(hidden, mixer_gain.reshape(1, D), value_proj, state_proj, decay, step))

    slices = lax.all_to_all(sent, "seq", split_axis=0, concat_axis=0, tiled=True)

    gate = pl.pallas_call(
        gate_kernel,
        grid=(blocks,),
        in_specs=[by_rows(Q, D), fixed_once(D, channels)],
        out_specs=by_rows(Q, channels),
        out_shape=stored(bf16, rows, channels),
        compiler_params=params(12),
        cost_estimate=cost(2 * rows * channels * D, 7 * 2**20),
        name="gate",
    )(*from_hbm(mixed, gate_proj))
    slices, gate = lax.optimization_barrier((slices, gate))

    before = pl.pallas_call(
        prefix_kernel,
        out_shape=shape_of(bf16, seq_count, slice_rows, channels),
        compiler_params=pltpu.CompilerParams(vmem_limit_bytes=8 * 2**20),
        name="prefix",
    )(slices)
    incoming = lax.all_to_all(before, "seq", split_axis=0, concat_axis=0, tiled=True)
    incoming = incoming.reshape(N, channels)

    within = pl.pallas_call(
        within_kernel,
        grid=(blocks,),
        in_specs=[
            by_rows(Q, channels),
            by_rows(Q, 2 * N),
            by_lanes(heads, Q),
            by_lanes(heads, Q),
            by_rows(1, N, channels),
            fixed(1, channels),
        ],
        out_specs=by_rows(Q, channels),
        out_shape=stored(f32, rows, channels),
        compiler_params=params(16),
        cost_estimate=cost(4 * rows * channels * Q, 6 * 2**20, rows * Q * heads),
        name="within",
    )(
        *from_hbm(x, maps, decay, step, enter),
        jnp.repeat(skip_gain, P_SIZE).reshape(1, channels),
    )

    incoming, within = lax.optimization_barrier((incoming, within))

    own, other = pl.pallas_call(
        normed_kernel,
        grid_spec=pltpu.PrefetchScalarGridSpec(
            num_scalar_prefetch=1,
            grid=(blocks,),
            in_specs=[
                by_rows(Q, channels),
                pl.BlockSpec((Q, N), lambda i, *_: (i, 1)),
                by_rows(Q, channels),
                by_lanes(heads, Q),
                fixed(N, channels),
                fixed(1, channels),
            ],
            out_specs=[by_rows(own_rows, channels), by_rows(own_rows, channels)],
            scratch_shapes=[pltpu.VMEM((heads, 128), f32)],
        ),
        out_shape=[shape_of(bf16, rows // 2, channels)] * 2,
        compiler_params=params(12),
        cost_estimate=cost(2 * rows * N * channels, 5 * 2**20),
        name="normed",
    )(
        core.reshape(1),
        *from_hbm(within, maps, gate, decay),
        incoming,
        group_gain.reshape(1, channels),
    )
    got = lax.ppermute(other, "exp", swap)

    at = jnp.stack([(line + hop) % lines for hop in range(lines)])

    def rows_of(hop):
        return pl.BlockSpec((own_rows, channels), lambda i, at: (at[hop], 0))

    def project(kernel, in_specs, out_specs, out_shape, share, name):
        return pl.pallas_call(
            kernel,
            grid_spec=pltpu.PrefetchScalarGridSpec(
                num_scalar_prefetch=1, grid=(1,), in_specs=in_specs, out_specs=out_specs
            ),
            out_shape=out_shape,
            compiler_params=params(10),
            cost_estimate=cost(share * own_rows * channels * D, 3 * 2**20),
            name=name,
        )

    half = fixed(own_rows, HALF)
    half_pair = [shape_of(bf16, own_rows, HALF)] * 2

    own_w = from_vmem(out_proj)
    part, got_w = project(
        own_part_kernel,
        [rows_of(2), resident(), fixed(channels, D)],
        [fixed(own_rows, D), resident()],
        [pltpu.VMEM((own_rows, D), f32), pltpu.VMEM((channels, D), bf16)],
        2,
        "own_part",
    )(at, own, *own_w, *from_hbm(other_proj))
    got, part = lax.optimization_barrier((got, part))
    projections = own_w + from_vmem(got_w)

    def halves(at, hop_a, hop_b, *arrived):
        return project(
            halves_kernel,
            [rows_of(hop_a), rows_of(hop_a), rows_of(hop_b), rows_of(hop_b)]
            + [resident(), resident()]
            + [half] * len(arrived),
            [half, half],
            half_pair,
            4,
            "halves",
        )(at, own, got, own, got, *projections, *arrived)

    def send(piece, hop):
        moves = [(i, (i + 2 * hop) % exp_count) for i in range(exp_count)]
        return lax.ppermute(piece, "exp", moves)

    far_left, far_right = project(
        finish_kernel,
        [fixed(own_rows, D), rows_of(2), resident()],
        [half, half],
        half_pair,
        2,
        "finish",
    )(at, part, got, projections[1])
    via_next, via_last = send(far_left, 1), send(far_right, 3)
    next_right, last_left = halves(at, 1, 3)
    right_pieces = [send(next_right, 1)]
    left_pieces = [send(last_left, 3)]
    next_left, last_right = halves(at, 1, 3, via_next, via_last)
    left_pieces.append(send(next_left, 1))
    right_pieces.append(send(last_right, 3))
    late_at, late_ids, _ = lax.optimization_barrier((at, expert_ids, next_left))
    mine_right, mine_left = halves(late_at, 0, 0)
    left_pieces.append(mine_left)
    right_pieces.append(mine_right)
    named, rank, picker = pl.pallas_call(
        route_kernel,
        grid=(4,),
        in_specs=[fixed(own_rows, expert_ids.shape[1])],
        out_specs=[
            fixed(own_rows, experts),
            fixed(own_rows, experts),
            by_rows(per_step, 2 * own_rows),
        ],
        out_shape=[
            shape_of(f32, own_rows, experts),
            shape_of(f32, own_rows, experts),
            stored(bf16, slab_rows, 2 * own_rows),
        ],
        scratch_shapes=[pltpu.VMEM((own_rows, experts), bf16)],
        compiler_params=params(12),
        cost_estimate=cost(2 * slab_rows * experts * own_rows, 4 * 2**20),
        name="route",
    )(late_ids)

    mixer_out, weight, outgoing = pl.pallas_call(
        dispatch_kernel,
        grid_spec=pltpu.PrefetchScalarGridSpec(
            num_scalar_prefetch=1,
            grid=(1,),
            in_specs=[fixed(own_rows, HALF)] * 6
            + [
                pl.BlockSpec((own_rows, D), lambda i, at: (at[0], 0)),
                fixed(1, D),
                fixed(D, experts),
                fixed(own_rows, experts),
                resident(),
            ],
            out_specs=[fixed(own_rows, D), fixed(own_rows, experts), resident()],
        ),
        out_shape=[
            shape_of(bf16, own_rows, D),
            shape_of(f32, own_rows, experts),
            pltpu.VMEM((slab_rows, HALF), bf16),
        ],
        compiler_params=params(24),
        cost_estimate=cost(4 * slab_rows * own_rows * HALF, 10 * 2**20),
        name="dispatch",
    )(
        place.reshape(1),
        *left_pieces,
        *right_pieces,
        *from_hbm(hidden, moe_gain.reshape(1, D), router),
        named,
        *from_vmem(picker),
    )

    arrived = lax.all_to_all(
        outgoing.reshape(peers, SLAB, HALF),
        ("seq", "exp"),
        split_axis=0,
        concat_axis=0,
        tiled=True,
    ).reshape(peers, 3, 8, HALF)
    group = peers // 4
    combine_weight = pl.pallas_call(
        combine_weight_kernel,
        grid=(4,),
        in_specs=[fixed(own_rows, experts), fixed(own_rows, experts)],
        out_specs=by_lanes(2 * own_rows, per_step),
        out_shape=pltpu.VMEM((2 * own_rows, slab_rows), bf16),
        compiler_params=params(12),
        cost_estimate=cost(4 * slab_rows * experts * own_rows, 4 * 2**20),
        name="combine_weight",
    )(rank, weight)

    def piece(index):
        return pl.BlockSpec((group, None, 8, HALF), lambda i: (i, index, 0, 0))

    results = pl.pallas_call(
        expert_kernel,
        grid=(4,),
        in_specs=[piece(0), piece(1), piece(2), resident(), resident()],
        out_specs=by_rows(group, 3, 8, HALF),
        out_shape=stored(bf16, peers, 3, 8, HALF),
        compiler_params=params(28),
        cost_estimate=cost(6 * peers * CAP * D * F, 22 * 2**20, peers * CAP * F),
        name="experts",
    )(arrived, arrived, arrived, *from_vmem(expert_gate_up, expert_down))
    returned = lax.all_to_all(
        results.reshape(peers, SLAB, HALF),
        ("seq", "exp"),
        split_axis=0,
        concat_axis=0,
        tiled=True,
    )

    layer_out = pl.pallas_call(
        combine_kernel,
        in_specs=[pl.BlockSpec(memory_space=pl.ANY), resident(), resident()],
        out_specs=resident(),
        out_shape=shape_of(bf16, own_rows, D),
        scratch_shapes=[
            pltpu.VMEM((8, peers // 8, SLAB, HALF), bf16),
            pltpu.SemaphoreType.DMA((8,)),
        ],
        compiler_params=pltpu.CompilerParams(vmem_limit_bytes=24 * 2**20),
        cost_estimate=cost(4 * slab_rows * own_rows * HALF, 8 * 2**20),
        name="combine",
    )(*from_hbm(returned), *from_vmem(combine_weight, mixer_out))
    return (mixer_out, layer_out)


def solution(mesh):
    in_specs = (
        P("seq", None),
        P(),
        P(None, "exp"),
        P(None, "exp"),
        P(None, "exp"),
        P("seq", "exp"),
        P("seq", "exp"),
        P("exp"),
        P("exp"),
        P("exp", None),
        P(),
        P(),
        P(("seq", "exp"), None),
        P(("seq", "exp"), None, None),
        P(("seq", "exp"), None, None),
    )
    out_specs = (P(("seq", "exp"), None), P(("seq", "exp"), None))
    return jax.shard_map(body, mesh=mesh, in_specs=in_specs, out_specs=out_specs, check_vma=False)
```

```python
import jax
import jax.numpy as jnp
from jax import lax
from jax.experimental import pallas as pl
from jax.experimental.pallas import tpu as pltpu
from jax.sharding import PartitionSpec as P

D = 2048
HALF = D // 2
P_SIZE = 64
N = 128
Q = 256
F = 768
CAP = 12
SLAB = 2 * CAP

f32 = jnp.float32
bf16 = jnp.bfloat16
epsilon = 1e-05
LOG2_E = 1.4426950408889634


def params(mib):
    return pltpu.CompilerParams(
        dimension_semantics=("arbitrary",), vmem_limit_bytes=mib * 2**20
    )


def cost(flops, nbytes, transcendentals=0):
    return pl.CostEstimate(
        flops=int(flops), bytes_accessed=int(nbytes), transcendentals=int(transcendentals)
    )


def iota(shape, axis, kind=jnp.int32):
    return lax.broadcasted_iota(jnp.int32, shape, axis).astype(kind)


def dot(a, b):
    return jnp.dot(a, b, preferred_element_type=f32)


def dot_first(a, b):
    return lax.dot_general(a, b, (((0,), (0,)), ((), ())), preferred_element_type=f32)


def dot_last(a, b):
    return lax.dot_general(a, b, (((1,), (1,)), ((), ())), preferred_element_type=f32)


def running_sum(rates):
    heads, count = rates.shape
    upper = (iota((count, count), 0) <= iota((count, count), 1)).astype(f32).astype(bf16)
    terms = []
    for _ in range(3):
        term = rates.astype(bf16)
        terms.append(term)
        rates = rates - term.astype(f32)
    sums = dot(jnp.concatenate(terms, axis=0), upper)
    return sums[:heads] + (sums[heads : 2 * heads] + sums[2 * heads :])


def per_channel(values):
    heads = values.shape[0]
    lanes = heads * P_SIZE
    first = iota((heads, lanes), 0) * P_SIZE
    lane = iota((heads, lanes), 1)
    spread = ((lane >= first) & (lane < first + P_SIZE)).astype(f32)
    coarse = values.astype(bf16).astype(f32)
    terms = jnp.concatenate([coarse, values - coarse], axis=0).astype(bf16)
    return dot_first(terms, jnp.concatenate([spread, spread], axis=0).astype(bf16))


def row_per_channel(column):
    return per_channel(jnp.broadcast_to(column, (column.shape[0], 128)))[0:1]


def local_state_kernel(
    hidden_ref,
    gain_ref,
    value_ref,
    state_ref,
    decay_ref,
    step_ref,
    mixed_ref,
    x_ref,
    maps_ref,
    enter_ref,
    sent_ref,
    state,
    total,
):
    block = pl.program_id(0)

    @pl.when(block == 0)
    def _():
        state[...] = jnp.zeros_like(state)
        total[...] = jnp.zeros_like(total)

    wide = hidden_ref[...].astype(f32)
    scale = lax.rsqrt(jnp.mean(wide * wide, axis=-1, keepdims=True) + epsilon)
    mixed = (wide * scale * gain_ref[...]).astype(bf16)
    mixed_ref[...] = mixed
    x = dot(mixed, value_ref[...]).astype(bf16)
    x_ref[...] = x
    maps = dot(mixed, state_ref[...]).astype(bf16)
    maps_ref[...] = maps
    sums = running_sum(decay_ref[...])
    end = sums[:, Q - 1 : Q]
    weight = per_channel(jnp.exp(end - sums) * step_ref[...])
    weighted = (x.astype(f32) * weight).astype(bf16)
    old = state[...]
    enter_ref[0] = old.astype(bf16)
    new = old * row_per_channel(jnp.exp(end)) + dot_first(maps[:, :N], weighted)
    state[...] = new
    total[...] = total[...] + end

    @pl.when(block == pl.num_programs(0) - 1)
    def _():
        parts = sent_ref.shape[0]
        channels = new.shape[1]
        log_total = row_per_channel(total[:, 0:1])
        coarse = log_total.astype(bf16).astype(f32)
        which = iota((8, channels), 0)
        tail = jnp.where(which == 0, coarse, jnp.where(which == 1, log_total - coarse, 0.0))
        rows = new.reshape(parts, N // parts, channels)
        sent_ref[...] = jnp.concatenate(
            [rows, jnp.broadcast_to(tail[None], (parts, 8, channels))], axis=1
        ).astype(bf16)


def prefix_kernel(got_ref, out_ref):
    count = got_ref.shape[0]
    rows = out_ref.shape[1]
    carry = jnp.zeros(out_ref.shape[1:], f32)
    for shard in range(count):
        out_ref[shard] = carry.astype(bf16)
        got = got_ref[shard].astype(f32)
        decay = jnp.exp(got[rows : rows + 1] + got[rows + 1 : rows + 2])
        carry = decay * carry + got[:rows]


def within_kernel(
    mixed_ref,
    gate_w_ref,
    x_ref,
    maps_ref,
    decay_ref,
    step_ref,
    enter_ref,
    skip_ref,
    *rest,
):
    gate_ref, within_ref = rest[-2:]
    gate_ref[...] = dot(mixed_ref[...], gate_w_ref[...]).astype(bf16)
    sums = running_sum(decay_ref[...])
    heads = sums.shape[0]
    maps = maps_ref[...]
    part = Q // 2
    scores = dot_last(maps[:, N:], maps[:, :N])
    from_start = per_channel(jnp.exp(sums)) * dot(maps[:, N:], enter_ref[0])
    scaled = sums * LOG2_E
    source = scaled - jnp.log2(step_ref[...])
    blank = jnp.zeros((128 - heads, Q), f32)
    target = jnp.concatenate([scaled, blank], axis=0).T
    causal = iota((part, part), 0) >= iota((part, part), 1)
    left = (iota((Q, 2 * P_SIZE), 1) < P_SIZE).astype(f32).astype(bf16)
    right = (iota((Q, 2 * P_SIZE), 1) >= P_SIZE).astype(f32).astype(bf16)
    for pair in range(heads // 2):
        top, bottom = [], []
        for head in (2 * pair, 2 * pair + 1):
            column = target[:, head : head + 1]
            row = source[head : head + 1]
            corner = jnp.where(causal, column[:part] - row[:, :part], -jnp.inf)
            top.append((scores[:part, :part] * jnp.exp2(corner)).astype(bf16))
            past = column[part:] - row[:, :part]
            bottom.append((scores[part:, :part] * jnp.exp2(past)).astype(bf16))
            corner = jnp.where(causal, column[part:] - row[:, part:], -jnp.inf)
            bottom.append((scores[part:, part:] * jnp.exp2(corner)).astype(bf16))
        lanes = slice(pair * 2 * P_SIZE, (pair + 1) * 2 * P_SIZE)
        x = x_ref[:, lanes]
        x_left, x_right = x * left, x * right
        skip = x.astype(f32) * skip_ref[:, lanes] + from_start[:, lanes]
        within_ref[:part, lanes] = skip[:part] + dot(
            jnp.concatenate(top, axis=1),
            jnp.concatenate([x_left[:part], x_right[:part]], axis=0),
        )
        within_ref[part:, lanes] = skip[part:] + dot(
            jnp.concatenate(bottom, axis=1), jnp.concatenate([x_left, x_right], axis=0)
        )


def normed_kernel(
    core_ref,
    within_ref,
    maps_ref,
    gate_ref,
    decay_ref,
    incoming_ref,
    gain_ref,
    own_ref,
    other_ref,
    before,
):
    block = pl.program_id(0)

    @pl.when(block == 0)
    def _():
        before[...] = jnp.zeros_like(before)

    sums = running_sum(decay_ref[...]) + before[:, 0:1]
    before[...] = jnp.broadcast_to(sums[:, Q - 1 : Q], before.shape)
    carried = per_channel(jnp.exp(sums)) * dot(maps_ref[...], incoming_ref[...])
    gate = gate_ref[...].astype(f32)
    gated = (within_ref[...] + carried) * (gate * jax.nn.sigmoid(gate))
    scale = lax.rsqrt(jnp.mean(gated * gated, axis=-1, keepdims=True) + epsilon)
    normed = gated * scale * gain_ref[...]
    rows = own_ref.shape[0]
    first, second = normed[:rows], normed[rows:]
    mine = core_ref[0] == 0
    own_ref[...] = jnp.where(mine, first, second).astype(bf16)
    other_ref[...] = jnp.where(mine, second, first).astype(bf16)


def own_part_kernel(at_ref, own_ref, own_w_ref, got_w_ref, part_ref, kept_ref):
    part_ref[...] = dot(own_ref[...], own_w_ref[...])
    kept_ref[...] = got_w_ref[...]


def finish_kernel(at_ref, part_ref, got_ref, got_w_ref, left_ref, right_ref):
    out = part_ref[...] + dot(got_ref[...], got_w_ref[...])
    left_ref[...] = out[:, :HALF].astype(bf16)
    right_ref[...] = out[:, HALF:].astype(bf16)


def halves_kernel(
    at_ref, own_a_ref, got_a_ref, own_b_ref, got_b_ref, own_w_ref, got_w_ref, *rest
):
    *more, a_ref, b_ref = rest
    halves = (slice(0, HALF), slice(HALF, D))
    if not more:
        halves = halves[::-1]
    a = dot(own_a_ref[...], own_w_ref[:, halves[0]]) + dot(got_a_ref[...], got_w_ref[:, halves[0]])
    b = dot(own_b_ref[...], own_w_ref[:, halves[1]]) + dot(got_b_ref[...], got_w_ref[:, halves[1]])
    if more:
        a = a + more[0][...].astype(f32)
        b = b + more[1][...].astype(f32)
    a_ref[...] = a.astype(bf16)
    b_ref[...] = b.astype(bf16)


def slots(row):
    place = row - SLAB * jnp.floor((row + 0.5) * (1.0 / SLAB))
    slot = jnp.where(place < 8, place, jnp.where(place < 20, place - 8, place - 12))
    second = ((place >= 8) & (place < 16)) | (place >= 20)
    return slot, second


def expert_of(block, rows, experts):
    gap = iota((rows, experts), 0) + block * rows - SLAB * iota((rows, experts), 1)
    return ((gap >= 0) & (gap < SLAB)).astype(f32).astype(bf16)


def route_kernel(ids_ref, named_ref, rank_ref, picker_ref, ranks):
    block = pl.program_id(0)
    tokens, experts = named_ref.shape

    @pl.when(block == 0)
    def _():
        lane = iota((tokens, experts), 1)
        named = jnp.zeros((tokens, experts), f32)
        for k in range(ids_ref.shape[1]):
            named = named + (ids_ref[:, k : k + 1] == lane).astype(f32)
        named_ref[...] = named
        earlier = (iota((tokens, tokens), 0) > iota((tokens, tokens), 1)).astype(f32)
        rank = dot(earlier.astype(bf16), named.astype(bf16))
        rank = jnp.where(named > 0.5, rank, -1.0)
        rank_ref[...] = rank
        ranks[...] = rank.astype(bf16)

    rows = picker_ref.shape[0]
    ranked = dot_last(expert_of(block, rows, experts), ranks[...])
    slot, second = slots(iota((rows, tokens), 0, f32))
    hit = (ranked == slot).astype(f32)
    picker_ref[:, :tokens] = jnp.where(second, 0.0, hit).astype(bf16)
    picker_ref[:, tokens:] = jnp.where(second, hit, 0.0).astype(bf16)


def dispatch_kernel(
    where_ref,
    left_a_ref,
    left_b_ref,
    left_c_ref,
    right_a_ref,
    right_b_ref,
    right_c_ref,
    hidden_ref,
    gain_ref,
    router_ref,
    named_ref,
    picker_ref,
    mixer_ref,
    weight_ref,
    out_ref,
):
    left = left_a_ref[...].astype(f32) + left_b_ref[...].astype(f32)
    right = right_a_ref[...].astype(f32) + right_b_ref[...].astype(f32)
    head_sum = jnp.concatenate(
        [left + left_c_ref[...].astype(f32), right + right_c_ref[...].astype(f32)], axis=1
    )
    mixer_out = (hidden_ref[...].astype(f32) + head_sum).astype(bf16)
    mixer_ref[...] = mixer_out
    wide = mixer_out.astype(f32)
    scale = lax.rsqrt(jnp.mean(wide * wide, axis=-1, keepdims=True) + epsilon)
    expert_input = (wide * scale * gain_ref[...]).astype(bf16)
    rows_in = jnp.concatenate([expert_input[:, :HALF], expert_input[:, HALF:]], axis=0)
    picked = named_ref[...] * jax.nn.sigmoid(dot(expert_input, router_ref[...]))
    weight_ref[...] = picked / jnp.sum(picked, axis=-1, keepdims=True)
    step = out_ref.shape[0] // 8
    for i in range(8):
        part = slice(i * step, (i + 1) * step)
        out_ref[part] = dot(picker_ref[part], rows_in).astype(bf16)


def expert_kernel(got_ref, up_ref, down_ref, out_ref):
    peers = out_ref.shape[0]
    group = pl.ds(pl.program_id(0) * peers, peers)
    rows = peers * 8
    part = rows // 2
    place = iota((rows, rows), 0)
    lane = iota((rows, rows), 1)

    def source(row):
        inner = row & (part - 1)
        return ((inner >> 2) << 3) + jnp.where(row >= part, 4, 0) + (inner & 3)

    apart = (source(place) == lane).astype(f32).astype(bf16)
    together = (place == source(lane)).astype(f32).astype(bf16)
    tail = dot(apart, got_ref[group, 2].reshape(rows, HALF)).astype(bf16)
    x0 = jnp.concatenate([got_ref[group, 0].reshape(rows, HALF), tail[:part]], axis=0)
    x1 = jnp.concatenate([got_ref[group, 1].reshape(rows, HALF), tail[part:]], axis=0)
    projected = dot(x0, up_ref[0, :HALF]) + dot(x1, up_ref[0, HALF:])
    gate = projected[:, :F]
    hidden = (gate * jax.nn.sigmoid(gate) * projected[:, F:]).astype(bf16)
    y0 = dot(hidden, down_ref[0, :, :HALF]).astype(bf16)
    y1 = dot(hidden, down_ref[0, :, HALF:]).astype(bf16)
    out_ref[:, 0] = y0[:rows].reshape(peers, 8, HALF)
    out_ref[:, 1] = y1[:rows].reshape(peers, 8, HALF)
    tail = jnp.concatenate([y0[rows:], y1[rows:]], axis=0)
    out_ref[:, 2] = dot(together, tail).astype(bf16).reshape(peers, 8, HALF)


def combine_weight_kernel(rank_ref, weight_ref, out_ref):
    block = pl.program_id(0)
    tokens, experts = rank_ref.shape
    rows = out_ref.shape[1]
    member = expert_of(block, rows, experts)
    ranked = dot_last(rank_ref[...].astype(bf16), member)
    weight = dot_last(weight_ref[...].astype(bf16), member)
    slot, second = slots(iota((tokens, rows), 1, f32))
    weight = jnp.where(ranked == slot, weight, 0.0)
    out_ref[:tokens] = jnp.where(second, 0.0, weight).astype(bf16)
    out_ref[tokens:] = jnp.where(second, weight, 0.0).astype(bf16)


def combine_kernel(got_ref, weight_ref, mixer_ref, out_ref, held, ready):
    tokens = mixer_ref.shape[0]
    parts, group = held.shape[0], held.shape[1]
    rows = group * SLAB

    def fetch(i):
        return pltpu.make_async_copy(
            got_ref.at[pl.ds(i * group, group)], held.at[i], ready.at[i]
        )

    for i in range(parts):
        fetch(i).start()
    total = jnp.zeros((2 * tokens, HALF), f32)
    for i in range(parts):
        fetch(i).wait()
        total += dot(weight_ref[:, i * rows : (i + 1) * rows], held[i].reshape(rows, HALF))
    out_ref[:, :HALF] = (mixer_ref[:, :HALF].astype(f32) + total[:tokens]).astype(bf16)
    out_ref[:, HALF:] = (mixer_ref[:, HALF:].astype(f32) + total[tokens:]).astype(bf16)


def fixed(*shape):
    return pl.BlockSpec(shape, lambda *_: (0,) * len(shape))


def fixed_once(*shape):
    return pl.BlockSpec(
        shape, lambda *_: (0,) * len(shape), pipeline_mode=pl.Buffered(1)
    )


def by_rows(*shape):
    rest = (0,) * (len(shape) - 1)
    return pl.BlockSpec(shape, lambda i, *_: (i, *rest))


def by_lanes(*shape):
    return pl.BlockSpec(shape, lambda i, *_: (0, i))


def resident():
    return pl.BlockSpec(memory_space=pltpu.VMEM)


def shape_of(kind, *shape):
    return jax.ShapeDtypeStruct(shape, kind)


def stored(kind, *shape):
    return pltpu.HBM(shape, kind)


def from_hbm(*arrays):
    return [pltpu.with_memory_space_constraint(a, pltpu.HBM) for a in arrays]


def from_vmem(*arrays):
    return [pltpu.with_memory_space_constraint(a, pltpu.VMEM) for a in arrays]


def body(
    hidden,
    mixer_gain,
    gate_proj,
    value_proj,
    state_proj,
    log_decay,
    step_size,
    skip_gain,
    group_gain,
    out_proj,
    moe_gain,
    router,
    expert_ids,
    expert_gate_up,
    expert_down,
):
    rows = hidden.shape[0]
    heads = log_decay.shape[1]
    channels = heads * P_SIZE
    blocks = rows // Q
    seq_count = lax.axis_size("seq")
    exp_count = lax.axis_size("exp")
    peers = seq_count * exp_count
    place = lax.axis_index("exp")
    core, line = place % 2, place // 2
    lines = exp_count // 2
    own_rows = rows // exp_count
    slice_rows = N // seq_count
    experts = router.shape[1]
    slab_rows = experts * SLAB
    per_step = slab_rows // 4

    swap = [(i, i ^ 1) for i in range(exp_count)]
    other_proj = lax.ppermute(out_proj, "exp", swap)
    decay = log_decay.T
    step = step_size.T

    mixed, x, maps, enter, sent = pl.pallas_call(
        local_state_kernel,
        grid=(blocks,),
        in_specs=[
            by_rows(Q, D),
            fixed(1, D),
            fixed_once(D, channels),
            fixed_once(D, 2 * N),
            by_lanes(heads, Q),
            by_lanes(heads, Q),
        ],
        out_specs=[
            by_rows(Q, D),
            by_rows(Q, channels),
            by_rows(Q, 2 * N),
            by_rows(1, N, channels),
            fixed(seq_count, slice_rows + 8, channels),
        ],
        out_shape=[
            stored(bf16, rows, D),
            stored(bf16, rows, channels),
            stored(bf16, rows, 2 * N),
            stored(bf16, blocks, N, channels),
            shape_of(bf16, seq_count, slice_rows + 8, channels),
        ],
        scratch_shapes=[pltpu.VMEM((N, channels), f32), pltpu.VMEM((heads, 128), f32)],
        compiler_params=params(24),
        cost_estimate=cost(2 * rows * D * (channels + 2 * N), 16 * 2**20),
        name="local_state",
    )(*from_hbm(hidden, mixer_gain.reshape(1, D), value_proj, state_proj, decay, step))

    slices = lax.all_to_all(sent, "seq", split_axis=0, concat_axis=0, tiled=True)

    gate_w = from_vmem(gate_proj)
    inside = from_hbm(mixed, x, maps, decay, step, enter)
    skip = jnp.repeat(skip_gain, P_SIZE).reshape(1, channels)
    half_blocks = blocks // 2

    def within_half(first, earlier):
        def block(*shape):
            return pl.BlockSpec(shape, lambda i: (i + first, *(0,) * (len(shape) - 1)))

        def lanes():
            return pl.BlockSpec((heads, Q), lambda i: (0, i + first))

        mixed, x, maps, decay, step, enter = inside
        return pl.pallas_call(
            within_kernel,
            grid=(half_blocks,),
            in_specs=[
                block(Q, D),
                resident(),
                block(Q, channels),
                block(Q, 2 * N),
                lanes(),
                lanes(),
                block(1, N, channels),
                fixed(1, channels),
            ]
            + [pl.BlockSpec(memory_space=pl.ANY)] * len(earlier),
            out_specs=[block(Q, channels), block(Q, channels)],
            out_shape=[stored(bf16, rows, channels), stored(f32, rows, channels)],
            input_output_aliases={8 + i: i for i in range(len(earlier))},
            compiler_params=params(20),
            cost_estimate=cost(rows * channels * (D + 2 * Q), 5 * 2**20, rows * Q * heads // 2),
            name="within",
        )(mixed, *gate_w, x, maps, decay, step, enter, skip, *earlier)

    gate, within = within_half(0, ())
    slices, gate, within = lax.optimization_barrier((slices, gate, within))

    before = pl.pallas_call(
        prefix_kernel,
        out_shape=shape_of(bf16, seq_count, slice_rows, channels),
        compiler_params=pltpu.CompilerParams(vmem_limit_bytes=8 * 2**20),
        name="prefix",
    )(slices)
    incoming = lax.all_to_all(before, "seq", split_axis=0, concat_axis=0, tiled=True)
    incoming = incoming.reshape(N, channels)

    gate, within = within_half(half_blocks, from_hbm(gate, within))
    incoming, gate, within = lax.optimization_barrier((incoming, gate, within))

    own, other = pl.pallas_call(
        normed_kernel,
        grid_spec=pltpu.PrefetchScalarGridSpec(
            num_scalar_prefetch=1,
            grid=(blocks,),
            in_specs=[
                by_rows(Q, channels),
                pl.BlockSpec((Q, N), lambda i, *_: (i, 1)),
                by_rows(Q, channels),
                by_lanes(heads, Q),
                fixed(N, channels),
                fixed(1, channels),
            ],
            out_specs=[by_rows(own_rows, channels), by_rows(own_rows, channels)],
            scratch_shapes=[pltpu.VMEM((heads, 128), f32)],
        ),
        out_shape=[shape_of(bf16, rows // 2, channels)] * 2,
        compiler_params=params(12),
        cost_estimate=cost(2 * rows * N * channels, 5 * 2**20),
        name="normed",
    )(
        core.reshape(1),
        *from_hbm(within, maps, gate, decay),
        incoming,
        group_gain.reshape(1, channels),
    )
    got = lax.ppermute(other, "exp", swap)

    at = jnp.stack([(line + hop) % lines for hop in range(lines)])

    def rows_of(hop):
        return pl.BlockSpec((own_rows, channels), lambda i, at: (at[hop], 0))

    def project(kernel, in_specs, out_specs, out_shape, share, name):
        return pl.pallas_call(
            kernel,
            grid_spec=pltpu.PrefetchScalarGridSpec(
                num_scalar_prefetch=1, grid=(1,), in_specs=in_specs, out_specs=out_specs
            ),
            out_shape=out_shape,
            compiler_params=params(10),
            cost_estimate=cost(share * own_rows * channels * D, 3 * 2**20),
            name=name,
        )

    half = fixed(own_rows, HALF)
    half_pair = [shape_of(bf16, own_rows, HALF)] * 2

    own_w = from_vmem(out_proj)
    part, got_w = project(
        own_part_kernel,
        [rows_of(2), resident(), fixed(channels, D)],
        [fixed(own_rows, D), resident()],
        [pltpu.VMEM((own_rows, D), f32), pltpu.VMEM((channels, D), bf16)],
        2,
        "own_part",
    )(at, own, *own_w, *from_hbm(other_proj))
    got, part = lax.optimization_barrier((got, part))
    projections = own_w + from_vmem(got_w)

    def halves(at, hop_a, hop_b, *arrived, kept=half_pair):
        return project(
            halves_kernel,
            [rows_of(hop_a), rows_of(hop_a), rows_of(hop_b), rows_of(hop_b)]
            + [resident(), resident()]
            + [half] * len(arrived),
            [half, half],
            kept,
            4,
            "halves",
        )(at, own, got, own, got, *projections, *arrived)

    def send(piece, hop):
        moves = [(i, (i + 2 * hop) % exp_count) for i in range(exp_count)]
        return lax.ppermute(piece, "exp", moves)

    far_left, far_right = project(
        finish_kernel,
        [fixed(own_rows, D), rows_of(2), resident()],
        [half, half],
        half_pair,
        2,
        "finish",
    )(at, part, got, projections[1])
    via_next, via_last = send(far_left, 1), send(far_right, 3)
    next_right, last_left = halves(at, 1, 3)
    later_at, _ = lax.optimization_barrier((at, next_right))
    mine_right, mine_left = from_hbm(
        *halves(later_at, 0, 0, kept=[stored(bf16, own_rows, HALF)] * 2)
    )
    next_right, last_left, mine_left, mine_right = lax.optimization_barrier(
        (next_right, last_left, mine_left, mine_right)
    )
    right_pieces = [send(next_right, 1), mine_right]
    left_pieces = [send(last_left, 3), mine_left]
    next_left, last_right = halves(at, 1, 3, via_next, via_last)
    left_pieces.append(send(next_left, 1))
    right_pieces.append(send(last_right, 3))
    late_ids, _ = lax.optimization_barrier((expert_ids, next_left))
    named, rank, picker = pl.pallas_call(
        route_kernel,
        grid=(4,),
        in_specs=[fixed(own_rows, expert_ids.shape[1])],
        out_specs=[
            fixed(own_rows, experts),
            fixed(own_rows, experts),
            by_rows(per_step, 2 * own_rows),
        ],
        out_shape=[
            shape_of(f32, own_rows, experts),
            shape_of(f32, own_rows, experts),
            pltpu.VMEM((slab_rows, 2 * own_rows), bf16),
        ],
        scratch_shapes=[pltpu.VMEM((own_rows, experts), bf16)],
        compiler_params=params(12),
        cost_estimate=cost(2 * slab_rows * experts * own_rows, 4 * 2**20),
        name="route",
    )(late_ids)

    mixer_out, weight, outgoing = pl.pallas_call(
        dispatch_kernel,
        grid_spec=pltpu.PrefetchScalarGridSpec(
            num_scalar_prefetch=1,
            grid=(1,),
            in_specs=[fixed(own_rows, HALF)] * 6
            + [
                pl.BlockSpec((own_rows, D), lambda i, at: (at[0], 0)),
                fixed(1, D),
                fixed(D, experts),
                fixed(own_rows, experts),
                resident(),
            ],
            out_specs=[fixed(own_rows, D), fixed(own_rows, experts), resident()],
        ),
        out_shape=[
            shape_of(bf16, own_rows, D),
            shape_of(f32, own_rows, experts),
            pltpu.VMEM((slab_rows, HALF), bf16),
        ],
        compiler_params=params(24),
        cost_estimate=cost(4 * slab_rows * own_rows * HALF, 10 * 2**20),
        name="dispatch",
    )(
        place.reshape(1),
        *left_pieces,
        *right_pieces,
        *from_hbm(hidden, moe_gain.reshape(1, D), router),
        named,
        *from_vmem(picker),
    )

    arrived = lax.all_to_all(
        outgoing.reshape(peers, SLAB, HALF),
        ("seq", "exp"),
        split_axis=0,
        concat_axis=0,
        tiled=True,
    ).reshape(peers, 3, 8, HALF)
    group = peers // 4
    combine_weight = pl.pallas_call(
        combine_weight_kernel,
        grid=(4,),
        in_specs=[fixed(own_rows, experts), fixed(own_rows, experts)],
        out_specs=by_lanes(2 * own_rows, per_step),
        out_shape=pltpu.VMEM((2 * own_rows, slab_rows), bf16),
        compiler_params=params(12),
        cost_estimate=cost(4 * slab_rows * experts * own_rows, 4 * 2**20),
        name="combine_weight",
    )(rank, weight)

    results = pl.pallas_call(
        expert_kernel,
        grid=(4,),
        in_specs=[resident()] * 3,
        out_specs=by_rows(group, 3, 8, HALF),
        out_shape=stored(bf16, peers, 3, 8, HALF),
        compiler_params=params(28),
        cost_estimate=cost(6 * peers * CAP * D * F, 22 * 2**20, peers * CAP * F),
        name="experts",
    )(*from_vmem(arrived, expert_gate_up, expert_down))
    returned = lax.all_to_all(
        results.reshape(peers, SLAB, HALF),
        ("seq", "exp"),
        split_axis=0,
        concat_axis=0,
        tiled=True,
    )

    layer_out = pl.pallas_call(
        combine_kernel,
        in_specs=[pl.BlockSpec(memory_space=pl.ANY), resident(), resident()],
        out_specs=resident(),
        out_shape=shape_of(bf16, own_rows, D),
        scratch_shapes=[
            pltpu.VMEM((8, peers // 8, SLAB, HALF), bf16),
            pltpu.SemaphoreType.DMA((8,)),
        ],
        compiler_params=pltpu.CompilerParams(vmem_limit_bytes=24 * 2**20),
        cost_estimate=cost(4 * slab_rows * own_rows * HALF, 8 * 2**20),
        name="combine",
    )(*from_hbm(returned), *from_vmem(combine_weight, mixer_out))
    return (mixer_out, layer_out)


def solution(mesh):
    in_specs = (
        P("seq", None),
        P(),
        P(None, "exp"),
        P(None, "exp"),
        P(None, "exp"),
        P("seq", "exp"),
        P("seq", "exp"),
        P("exp"),
        P("exp"),
        P("exp", None),
        P(),
        P(),
        P(("seq", "exp"), None),
        P(("seq", "exp"), None, None),
        P(("seq", "exp"), None, None),
    )
    out_specs = (P(("seq", "exp"), None), P(("seq", "exp"), None))
    return jax.shard_map(body, mesh=mesh, in_specs=in_specs, out_specs=out_specs, check_vma=False)
```

```python
import jax
import jax.numpy as jnp
from jax import lax
from jax.experimental import pallas as pl
from jax.experimental.pallas import tpu as pltpu
from jax.sharding import PartitionSpec as P

D = 2048
HALF = D // 2
P_SIZE = 64
N = 128
Q = 256
F = 768
CAP = 12
SLAB = 2 * CAP

f32 = jnp.float32
bf16 = jnp.bfloat16
epsilon = 1e-05
LOG2_E = 1.4426950408889634


def params(mib):
    return pltpu.CompilerParams(
        dimension_semantics=("arbitrary",), vmem_limit_bytes=mib * 2**20
    )


def cost(flops, nbytes, transcendentals=0):
    return pl.CostEstimate(
        flops=int(flops), bytes_accessed=int(nbytes), transcendentals=int(transcendentals)
    )


def iota(shape, axis, kind=jnp.int32):
    return lax.broadcasted_iota(jnp.int32, shape, axis).astype(kind)


def dot(a, b):
    return jnp.dot(a, b, preferred_element_type=f32)


def dot_first(a, b):
    return lax.dot_general(a, b, (((0,), (0,)), ((), ())), preferred_element_type=f32)


def dot_last(a, b):
    return lax.dot_general(a, b, (((1,), (1,)), ((), ())), preferred_element_type=f32)


def running_sum(rates):
    heads, count = rates.shape
    upper = (iota((count, count), 0) <= iota((count, count), 1)).astype(f32).astype(bf16)
    terms = []
    for _ in range(3):
        term = rates.astype(bf16)
        terms.append(term)
        rates = rates - term.astype(f32)
    sums = dot(jnp.concatenate(terms, axis=0), upper)
    return sums[:heads] + (sums[heads : 2 * heads] + sums[2 * heads :])


def per_channel(values):
    heads = values.shape[0]
    lanes = heads * P_SIZE
    first = iota((heads, lanes), 0) * P_SIZE
    lane = iota((heads, lanes), 1)
    spread = ((lane >= first) & (lane < first + P_SIZE)).astype(f32)
    coarse = values.astype(bf16).astype(f32)
    terms = jnp.concatenate([coarse, values - coarse], axis=0).astype(bf16)
    return dot_first(terms, jnp.concatenate([spread, spread], axis=0).astype(bf16))


def row_per_channel(column):
    return per_channel(jnp.broadcast_to(column, (column.shape[0], 128)))[0:1]


def local_state_kernel(
    hidden_ref,
    gain_ref,
    value_ref,
    state_ref,
    decay_ref,
    step_ref,
    mixed_ref,
    x_ref,
    maps_ref,
    enter_ref,
    sent_ref,
    state,
    total,
):
    block = pl.program_id(0)

    @pl.when(block == 0)
    def _():
        state[...] = jnp.zeros_like(state)
        total[...] = jnp.zeros_like(total)

    wide = hidden_ref[...].astype(f32)
    scale = lax.rsqrt(jnp.mean(wide * wide, axis=-1, keepdims=True) + epsilon)
    mixed = (wide * scale * gain_ref[...]).astype(bf16)
    mixed_ref[...] = mixed
    x = dot(mixed, value_ref[...]).astype(bf16)
    x_ref[...] = x
    maps = dot(mixed, state_ref[...]).astype(bf16)
    maps_ref[...] = maps
    sums = running_sum(decay_ref[...])
    end = sums[:, Q - 1 : Q]
    weight = per_channel(jnp.exp(end - sums) * step_ref[...])
    weighted = (x.astype(f32) * weight).astype(bf16)
    old = state[...]
    enter_ref[0] = old.astype(bf16)
    new = old * row_per_channel(jnp.exp(end)) + dot_first(maps[:, :N], weighted)
    state[...] = new
    total[...] = total[...] + end

    @pl.when(block == pl.num_programs(0) - 1)
    def _():
        parts = sent_ref.shape[0]
        channels = new.shape[1]
        log_total = row_per_channel(total[:, 0:1])
        coarse = log_total.astype(bf16).astype(f32)
        which = iota((8, channels), 0)
        tail = jnp.where(which == 0, coarse, jnp.where(which == 1, log_total - coarse, 0.0))
        rows = new.reshape(parts, N // parts, channels)
        sent_ref[...] = jnp.concatenate(
            [rows, jnp.broadcast_to(tail[None], (parts, 8, channels))], axis=1
        ).astype(bf16)


def prefix_kernel(got_ref, out_ref):
    count = got_ref.shape[0]
    rows = out_ref.shape[1]
    carry = jnp.zeros(out_ref.shape[1:], f32)
    for shard in range(count):
        out_ref[shard] = carry.astype(bf16)
        got = got_ref[shard].astype(f32)
        decay = jnp.exp(got[rows : rows + 1] + got[rows + 1 : rows + 2])
        carry = decay * carry + got[:rows]


def within_kernel(
    mixed_ref,
    gate_w_ref,
    x_ref,
    maps_ref,
    decay_ref,
    step_ref,
    enter_ref,
    skip_ref,
    *rest,
):
    gate_ref, within_ref = rest[-2:]
    gate_ref[...] = dot(mixed_ref[...], gate_w_ref[...]).astype(bf16)
    sums = running_sum(decay_ref[...])
    heads = sums.shape[0]
    maps = maps_ref[...]
    part = Q // 2
    scores = dot_last(maps[:, N:], maps[:, :N])
    from_start = per_channel(jnp.exp(sums)) * dot(maps[:, N:], enter_ref[0])
    scaled = sums * LOG2_E
    source = scaled - jnp.log2(step_ref[...])
    blank = jnp.zeros((128 - heads, Q), f32)
    target = jnp.concatenate([scaled, blank], axis=0).T
    causal = iota((part, part), 0) >= iota((part, part), 1)
    left = (iota((Q, 2 * P_SIZE), 1) < P_SIZE).astype(f32).astype(bf16)
    right = (iota((Q, 2 * P_SIZE), 1) >= P_SIZE).astype(f32).astype(bf16)
    for pair in range(heads // 2):
        top, bottom = [], []
        for head in (2 * pair, 2 * pair + 1):
            column = target[:, head : head + 1]
            row = source[head : head + 1]
            corner = jnp.where(causal, column[:part] - row[:, :part], -jnp.inf)
            top.append((scores[:part, :part] * jnp.exp2(corner)).astype(bf16))
            past = column[part:] - row[:, :part]
            bottom.append((scores[part:, :part] * jnp.exp2(past)).astype(bf16))
            corner = jnp.where(causal, column[part:] - row[:, part:], -jnp.inf)
            bottom.append((scores[part:, part:] * jnp.exp2(corner)).astype(bf16))
        lanes = slice(pair * 2 * P_SIZE, (pair + 1) * 2 * P_SIZE)
        x = x_ref[:, lanes]
        x_left, x_right = x * left, x * right
        skip = x.astype(f32) * skip_ref[:, lanes] + from_start[:, lanes]
        within_ref[:part, lanes] = skip[:part] + dot(
            jnp.concatenate(top, axis=1),
            jnp.concatenate([x_left[:part], x_right[:part]], axis=0),
        )
        within_ref[part:, lanes] = skip[part:] + dot(
            jnp.concatenate(bottom, axis=1), jnp.concatenate([x_left, x_right], axis=0)
        )


def normed_kernel(
    core_ref,
    within_ref,
    maps_ref,
    gate_ref,
    decay_ref,
    incoming_ref,
    gain_ref,
    own_ref,
    other_ref,
    before,
):
    block = pl.program_id(0)

    @pl.when(block == 0)
    def _():
        before[...] = jnp.zeros_like(before)

    sums = running_sum(decay_ref[...]) + before[:, 0:1]
    before[...] = jnp.broadcast_to(sums[:, Q - 1 : Q], before.shape)
    carried = per_channel(jnp.exp(sums)) * dot(maps_ref[...], incoming_ref[...])
    gate = gate_ref[...].astype(f32)
    gated = (within_ref[...] + carried) * (gate * jax.nn.sigmoid(gate))
    scale = lax.rsqrt(jnp.mean(gated * gated, axis=-1, keepdims=True) + epsilon)
    normed = gated * scale * gain_ref[...]
    rows = own_ref.shape[0]
    first, second = normed[:rows], normed[rows:]
    mine = core_ref[0] == 0
    own_ref[...] = jnp.where(mine, first, second).astype(bf16)
    other_ref[...] = jnp.where(mine, second, first).astype(bf16)


def own_part_kernel(at_ref, own_ref, own_w_ref, got_w_ref, part_ref, kept_ref, ready):
    keep = pltpu.make_async_copy(got_w_ref, kept_ref, ready)
    keep.start()
    part_ref[...] = dot(own_ref[...], own_w_ref[...])
    keep.wait()


def finish_kernel(at_ref, part_ref, got_ref, got_w_ref, left_ref, right_ref):
    out = part_ref[...] + dot(got_ref[...], got_w_ref[...])
    left_ref[...] = out[:, :HALF].astype(bf16)
    right_ref[...] = out[:, HALF:].astype(bf16)


def halves_kernel(
    at_ref, own_a_ref, got_a_ref, own_b_ref, got_b_ref, own_w_ref, got_w_ref, *rest
):
    *more, a_ref, b_ref = rest
    halves = (slice(0, HALF), slice(HALF, D))
    if not more:
        halves = halves[::-1]
    a = dot(own_a_ref[...], own_w_ref[:, halves[0]]) + dot(got_a_ref[...], got_w_ref[:, halves[0]])
    b = dot(own_b_ref[...], own_w_ref[:, halves[1]]) + dot(got_b_ref[...], got_w_ref[:, halves[1]])
    if more:
        a = a + more[0][...].astype(f32)
        b = b + more[1][...].astype(f32)
    a_ref[...] = a.astype(bf16)
    b_ref[...] = b.astype(bf16)


def slots(row):
    place = row - SLAB * jnp.floor((row + 0.5) * (1.0 / SLAB))
    slot = jnp.where(place < 8, place, jnp.where(place < 20, place - 8, place - 12))
    second = ((place >= 8) & (place < 16)) | (place >= 20)
    return slot, second


def expert_of(block, rows, experts):
    gap = iota((rows, experts), 0) + block * rows - SLAB * iota((rows, experts), 1)
    return ((gap >= 0) & (gap < SLAB)).astype(f32).astype(bf16)


def route_kernel(ids_ref, named_ref, rank_ref, picker_ref, ranks):
    block = pl.program_id(0)
    tokens, experts = named_ref.shape

    @pl.when(block == 0)
    def _():
        lane = iota((tokens, experts), 1)
        named = jnp.zeros((tokens, experts), f32)
        for k in range(ids_ref.shape[1]):
            named = named + (ids_ref[:, k : k + 1] == lane).astype(f32)
        named_ref[...] = named
        earlier = (iota((tokens, tokens), 0) > iota((tokens, tokens), 1)).astype(f32)
        rank = dot(earlier.astype(bf16), named.astype(bf16))
        rank = jnp.where(named > 0.5, rank, -1.0)
        rank_ref[...] = rank
        ranks[...] = rank.astype(bf16)

    rows = picker_ref.shape[0]
    ranked = dot_last(expert_of(block, rows, experts), ranks[...])
    slot, second = slots(iota((rows, tokens), 0, f32))
    hit = (ranked == slot).astype(f32)
    picker_ref[:, :tokens] = jnp.where(second, 0.0, hit).astype(bf16)
    picker_ref[:, tokens:] = jnp.where(second, hit, 0.0).astype(bf16)


def dispatch_kernel(
    where_ref,
    left_a_ref,
    left_b_ref,
    left_c_ref,
    right_a_ref,
    right_b_ref,
    right_c_ref,
    hidden_ref,
    gain_ref,
    router_ref,
    named_ref,
    picker_ref,
    mixer_ref,
    weight_ref,
    out_ref,
):
    left = left_a_ref[...].astype(f32) + left_b_ref[...].astype(f32)
    right = right_a_ref[...].astype(f32) + right_b_ref[...].astype(f32)
    head_sum = jnp.concatenate(
        [left + left_c_ref[...].astype(f32), right + right_c_ref[...].astype(f32)], axis=1
    )
    mixer_out = (hidden_ref[...].astype(f32) + head_sum).astype(bf16)
    mixer_ref[...] = mixer_out
    wide = mixer_out.astype(f32)
    scale = lax.rsqrt(jnp.mean(wide * wide, axis=-1, keepdims=True) + epsilon)
    expert_input = (wide * scale * gain_ref[...]).astype(bf16)
    rows_in = jnp.concatenate([expert_input[:, :HALF], expert_input[:, HALF:]], axis=0)
    picked = named_ref[...] * jax.nn.sigmoid(dot(expert_input, router_ref[...]))
    weight_ref[...] = picked / jnp.sum(picked, axis=-1, keepdims=True)
    step = out_ref.shape[0] // 8
    for i in range(8):
        part = slice(i * step, (i + 1) * step)
        out_ref[part] = dot(picker_ref[part], rows_in).astype(bf16)


def expert_kernel(got_ref, up_ref, down_ref, out_ref):
    peers = out_ref.shape[0]
    group = pl.ds(pl.program_id(0) * peers, peers)
    rows = peers * 8
    part = rows // 2
    place = iota((rows, rows), 0)
    lane = iota((rows, rows), 1)

    def source(row):
        inner = row & (part - 1)
        return ((inner >> 2) << 3) + jnp.where(row >= part, 4, 0) + (inner & 3)

    apart = (source(place) == lane).astype(f32).astype(bf16)
    together = (place == source(lane)).astype(f32).astype(bf16)
    tail = dot(apart, got_ref[group, 2].reshape(rows, HALF)).astype(bf16)
    x0 = jnp.concatenate([got_ref[group, 0].reshape(rows, HALF), tail[:part]], axis=0)
    x1 = jnp.concatenate([got_ref[group, 1].reshape(rows, HALF), tail[part:]], axis=0)
    projected = dot(x0, up_ref[0, :HALF]) + dot(x1, up_ref[0, HALF:])
    gate = projected[:, :F]
    hidden = (gate * jax.nn.sigmoid(gate) * projected[:, F:]).astype(bf16)
    y0 = dot(hidden, down_ref[0, :, :HALF]).astype(bf16)
    y1 = dot(hidden, down_ref[0, :, HALF:]).astype(bf16)
    out_ref[:, 0] = y0[:rows].reshape(peers, 8, HALF)
    out_ref[:, 1] = y1[:rows].reshape(peers, 8, HALF)
    tail = jnp.concatenate([y0[rows:], y1[rows:]], axis=0)
    out_ref[:, 2] = dot(together, tail).astype(bf16).reshape(peers, 8, HALF)


def combine_weight_kernel(rank_ref, weight_ref, out_ref):
    block = pl.program_id(0)
    tokens, experts = rank_ref.shape
    rows = out_ref.shape[1]
    member = expert_of(block, rows, experts)
    ranked = dot_last(rank_ref[...].astype(bf16), member)
    weight = dot_last(weight_ref[...].astype(bf16), member)
    slot, second = slots(iota((tokens, rows), 1, f32))
    weight = jnp.where(ranked == slot, weight, 0.0)
    out_ref[:tokens] = jnp.where(second, 0.0, weight).astype(bf16)
    out_ref[tokens:] = jnp.where(second, weight, 0.0).astype(bf16)


def combine_kernel(got_ref, weight_ref, mixer_ref, out_ref, held, ready):
    tokens = mixer_ref.shape[0]
    parts, group = held.shape[0], held.shape[1]
    rows = group * SLAB

    def fetch(i):
        return pltpu.make_async_copy(
            got_ref.at[pl.ds(i * group, group)], held.at[i], ready.at[i]
        )

    for i in range(parts):
        fetch(i).start()
    total = jnp.zeros((2 * tokens, HALF), f32)
    for i in range(parts):
        fetch(i).wait()
        total += dot(weight_ref[:, i * rows : (i + 1) * rows], held[i].reshape(rows, HALF))
    out_ref[:, :HALF] = (mixer_ref[:, :HALF].astype(f32) + total[:tokens]).astype(bf16)
    out_ref[:, HALF:] = (mixer_ref[:, HALF:].astype(f32) + total[tokens:]).astype(bf16)


def fixed(*shape):
    return pl.BlockSpec(shape, lambda *_: (0,) * len(shape))


def fixed_once(*shape):
    return pl.BlockSpec(
        shape, lambda *_: (0,) * len(shape), pipeline_mode=pl.Buffered(1)
    )


def by_rows(*shape):
    rest = (0,) * (len(shape) - 1)
    return pl.BlockSpec(shape, lambda i, *_: (i, *rest))


def by_lanes(*shape):
    return pl.BlockSpec(shape, lambda i, *_: (0, i))


def resident():
    return pl.BlockSpec(memory_space=pltpu.VMEM)


def shape_of(kind, *shape):
    return jax.ShapeDtypeStruct(shape, kind)


def stored(kind, *shape):
    return pltpu.HBM(shape, kind)


def from_hbm(*arrays):
    return [pltpu.with_memory_space_constraint(a, pltpu.HBM) for a in arrays]


def from_vmem(*arrays):
    return [pltpu.with_memory_space_constraint(a, pltpu.VMEM) for a in arrays]


def body(
    hidden,
    mixer_gain,
    gate_proj,
    value_proj,
    state_proj,
    log_decay,
    step_size,
    skip_gain,
    group_gain,
    out_proj,
    moe_gain,
    router,
    expert_ids,
    expert_gate_up,
    expert_down,
):
    rows = hidden.shape[0]
    heads = log_decay.shape[1]
    channels = heads * P_SIZE
    blocks = rows // Q
    seq_count = lax.axis_size("seq")
    exp_count = lax.axis_size("exp")
    peers = seq_count * exp_count
    place = lax.axis_index("exp")
    core, line = place % 2, place // 2
    lines = exp_count // 2
    own_rows = rows // exp_count
    slice_rows = N // seq_count
    experts = router.shape[1]
    slab_rows = experts * SLAB
    per_step = slab_rows // 4

    swap = [(i, i ^ 1) for i in range(exp_count)]
    other_proj = lax.ppermute(out_proj, "exp", swap)
    decay = log_decay.T
    step = step_size.T

    mixed, x, maps, enter, sent = pl.pallas_call(
        local_state_kernel,
        grid=(blocks,),
        in_specs=[
            by_rows(Q, D),
            fixed(1, D),
            fixed_once(D, channels),
            fixed_once(D, 2 * N),
            by_lanes(heads, Q),
            by_lanes(heads, Q),
        ],
        out_specs=[
            by_rows(Q, D),
            by_rows(Q, channels),
            by_rows(Q, 2 * N),
            by_rows(1, N, channels),
            fixed(seq_count, slice_rows + 8, channels),
        ],
        out_shape=[
            stored(bf16, rows, D),
            stored(bf16, rows, channels),
            stored(bf16, rows, 2 * N),
            stored(bf16, blocks, N, channels),
            shape_of(bf16, seq_count, slice_rows + 8, channels),
        ],
        scratch_shapes=[pltpu.VMEM((N, channels), f32), pltpu.VMEM((heads, 128), f32)],
        compiler_params=params(24),
        cost_estimate=cost(2 * rows * D * (channels + 2 * N), 16 * 2**20),
        name="local_state",
    )(*from_hbm(hidden, mixer_gain.reshape(1, D), value_proj, state_proj, decay, step))

    slices = lax.all_to_all(sent, "seq", split_axis=0, concat_axis=0, tiled=True)

    gate_w = from_vmem(gate_proj)
    inside = from_hbm(mixed, x, maps, decay, step, enter)
    skip = jnp.repeat(skip_gain, P_SIZE).reshape(1, channels)
    half_blocks = blocks // 2

    def within_half(first, earlier):
        def block(*shape):
            return pl.BlockSpec(shape, lambda i: (i + first, *(0,) * (len(shape) - 1)))

        def lanes():
            return pl.BlockSpec((heads, Q), lambda i: (0, i + first))

        mixed, x, maps, decay, step, enter = inside
        return pl.pallas_call(
            within_kernel,
            grid=(half_blocks,),
            in_specs=[
                block(Q, D),
                resident(),
                block(Q, channels),
                block(Q, 2 * N),
                lanes(),
                lanes(),
                block(1, N, channels),
                fixed(1, channels),
            ]
            + [pl.BlockSpec(memory_space=pl.ANY)] * len(earlier),
            out_specs=[block(Q, channels), block(Q, channels)],
            out_shape=[stored(bf16, rows, channels), stored(f32, rows, channels)],
            input_output_aliases={8 + i: i for i in range(len(earlier))},
            compiler_params=params(20),
            cost_estimate=cost(rows * channels * (D + 2 * Q), 5 * 2**20, rows * Q * heads // 2),
            name="within",
        )(mixed, *gate_w, x, maps, decay, step, enter, skip, *earlier)

    gate, within = within_half(0, ())
    slices, gate, within = lax.optimization_barrier((slices, gate, within))

    before = pl.pallas_call(
        prefix_kernel,
        out_shape=shape_of(bf16, seq_count, slice_rows, channels),
        compiler_params=pltpu.CompilerParams(vmem_limit_bytes=8 * 2**20),
        name="prefix",
    )(slices)
    incoming = lax.all_to_all(before, "seq", split_axis=0, concat_axis=0, tiled=True)
    incoming = incoming.reshape(N, channels)

    gate, within = within_half(half_blocks, from_hbm(gate, within))
    incoming, gate, within = lax.optimization_barrier((incoming, gate, within))

    own, other = pl.pallas_call(
        normed_kernel,
        grid_spec=pltpu.PrefetchScalarGridSpec(
            num_scalar_prefetch=1,
            grid=(blocks,),
            in_specs=[
                by_rows(Q, channels),
                pl.BlockSpec((Q, N), lambda i, *_: (i, 1)),
                by_rows(Q, channels),
                by_lanes(heads, Q),
                fixed(N, channels),
                fixed(1, channels),
            ],
            out_specs=[by_rows(own_rows, channels), by_rows(own_rows, channels)],
            scratch_shapes=[pltpu.VMEM((heads, 128), f32)],
        ),
        out_shape=[shape_of(bf16, rows // 2, channels)] * 2,
        compiler_params=params(12),
        cost_estimate=cost(2 * rows * N * channels, 5 * 2**20),
        name="normed",
    )(
        core.reshape(1),
        *from_hbm(within, maps, gate, decay),
        incoming,
        group_gain.reshape(1, channels),
    )
    got = lax.ppermute(other, "exp", swap)

    at = jnp.stack([(line + hop) % lines for hop in range(lines)])

    def rows_of(hop):
        return pl.BlockSpec((own_rows, channels), lambda i, at: (at[hop], 0))

    def project(kernel, in_specs, out_specs, out_shape, share, name, scratch=()):
        return pl.pallas_call(
            kernel,
            grid_spec=pltpu.PrefetchScalarGridSpec(
                num_scalar_prefetch=1,
                grid=(1,),
                in_specs=in_specs,
                out_specs=out_specs,
                scratch_shapes=scratch,
            ),
            out_shape=out_shape,
            compiler_params=params(10),
            cost_estimate=cost(share * own_rows * channels * D, 3 * 2**20),
            name=name,
        )

    half = fixed(own_rows, HALF)
    half_pair = [shape_of(bf16, own_rows, HALF)] * 2

    own_w = from_vmem(out_proj)
    part, got_w = project(
        own_part_kernel,
        [rows_of(2), resident(), pl.BlockSpec(memory_space=pl.ANY)],
        [fixed(own_rows, D), resident()],
        [pltpu.VMEM((own_rows, D), f32), pltpu.VMEM((channels, D), bf16)],
        2,
        "own_part",
        [pltpu.SemaphoreType.DMA],
    )(at, own, *own_w, *from_hbm(other_proj))
    got, part = lax.optimization_barrier((got, part))
    projections = own_w + from_vmem(got_w)

    def halves(at, hop_a, hop_b, *arrived, kept=half_pair):
        return project(
            halves_kernel,
            [rows_of(hop_a), rows_of(hop_a), rows_of(hop_b), rows_of(hop_b)]
            + [resident(), resident()]
            + [half] * len(arrived),
            [half, half],
            kept,
            4,
            "halves",
        )(at, own, got, own, got, *projections, *arrived)

    def send(piece, hop):
        moves = [(i, (i + 2 * hop) % exp_count) for i in range(exp_count)]
        return lax.ppermute(piece, "exp", moves)

    far_left, far_right = project(
        finish_kernel,
        [fixed(own_rows, D), rows_of(2), resident()],
        [half, half],
        half_pair,
        2,
        "finish",
    )(at, part, got, projections[1])
    via_next, via_last = send(far_left, 1), send(far_right, 3)
    next_right, last_left = halves(at, 1, 3)
    later_at, _ = lax.optimization_barrier((at, next_right))
    mine_right, mine_left = from_hbm(
        *halves(later_at, 0, 0, kept=[stored(bf16, own_rows, HALF)] * 2)
    )
    next_right, last_left, mine_left, mine_right = lax.optimization_barrier(
        (next_right, last_left, mine_left, mine_right)
    )
    right_pieces = [send(next_right, 1), mine_right]
    left_pieces = [send(last_left, 3), mine_left]
    next_left, last_right = halves(at, 1, 3, via_next, via_last)
    left_pieces.append(send(next_left, 1))
    right_pieces.append(send(last_right, 3))
    late_ids, _ = lax.optimization_barrier((expert_ids, next_left))
    named, rank, picker = pl.pallas_call(
        route_kernel,
        grid=(4,),
        in_specs=[fixed(own_rows, expert_ids.shape[1])],
        out_specs=[
            fixed(own_rows, experts),
            fixed(own_rows, experts),
            by_rows(per_step, 2 * own_rows),
        ],
        out_shape=[
            shape_of(f32, own_rows, experts),
            shape_of(f32, own_rows, experts),
            pltpu.VMEM((slab_rows, 2 * own_rows), bf16),
        ],
        scratch_shapes=[pltpu.VMEM((own_rows, experts), bf16)],
        compiler_params=params(12),
        cost_estimate=cost(2 * slab_rows * experts * own_rows, 4 * 2**20),
        name="route",
    )(late_ids)

    mixer_out, weight, outgoing = pl.pallas_call(
        dispatch_kernel,
        grid_spec=pltpu.PrefetchScalarGridSpec(
            num_scalar_prefetch=1,
            grid=(1,),
            in_specs=[resident()] * 6
            + [
                pl.BlockSpec((own_rows, D), lambda i, at: (at[0], 0)),
                fixed(1, D),
                fixed(D, experts),
                resident(),
                resident(),
            ],
            out_specs=[fixed(own_rows, D), fixed(own_rows, experts), resident()],
        ),
        out_shape=[
            shape_of(bf16, own_rows, D),
            shape_of(f32, own_rows, experts),
            pltpu.VMEM((slab_rows, HALF), bf16),
        ],
        compiler_params=params(24),
        cost_estimate=cost(4 * slab_rows * own_rows * HALF, 10 * 2**20),
        name="dispatch",
    )(
        place.reshape(1),
        *left_pieces,
        *right_pieces,
        *from_hbm(hidden, moe_gain.reshape(1, D), router),
        named,
        *from_vmem(picker),
    )

    arrived = lax.all_to_all(
        outgoing.reshape(peers, SLAB, HALF),
        ("seq", "exp"),
        split_axis=0,
        concat_axis=0,
        tiled=True,
    ).reshape(peers, 3, 8, HALF)
    group = peers // 4
    combine_weight = pl.pallas_call(
        combine_weight_kernel,
        grid=(4,),
        in_specs=[fixed(own_rows, experts), fixed(own_rows, experts)],
        out_specs=by_lanes(2 * own_rows, per_step),
        out_shape=pltpu.VMEM((2 * own_rows, slab_rows), bf16),
        compiler_params=params(12),
        cost_estimate=cost(4 * slab_rows * experts * own_rows, 4 * 2**20),
        name="combine_weight",
    )(rank, weight)

    results = pl.pallas_call(
        expert_kernel,
        grid=(4,),
        in_specs=[resident()] * 3,
        out_specs=by_rows(group, 3, 8, HALF),
        out_shape=stored(bf16, peers, 3, 8, HALF),
        compiler_params=params(28),
        cost_estimate=cost(6 * peers * CAP * D * F, 22 * 2**20, peers * CAP * F),
        name="experts",
    )(*from_vmem(arrived, expert_gate_up, expert_down))
    returned = lax.all_to_all(
        results.reshape(peers, SLAB, HALF),
        ("seq", "exp"),
        split_axis=0,
        concat_axis=0,
        tiled=True,
    )

    layer_out = pl.pallas_call(
        combine_kernel,
        in_specs=[pl.BlockSpec(memory_space=pl.ANY), resident(), resident()],
        out_specs=resident(),
        out_shape=shape_of(bf16, own_rows, D),
        scratch_shapes=[
            pltpu.VMEM((8, peers // 8, SLAB, HALF), bf16),
            pltpu.SemaphoreType.DMA((8,)),
        ],
        compiler_params=pltpu.CompilerParams(vmem_limit_bytes=24 * 2**20),
        cost_estimate=cost(4 * slab_rows * own_rows * HALF, 8 * 2**20),
        name="combine",
    )(*from_hbm(returned), *from_vmem(combine_weight, mixer_out))
    return (mixer_out, layer_out)


def solution(mesh):
    in_specs = (
        P("seq", None),
        P(),
        P(None, "exp"),
        P(None, "exp"),
        P(None, "exp"),
        P("seq", "exp"),
        P("seq", "exp"),
        P("exp"),
        P("exp"),
        P("exp", None),
        P(),
        P(),
        P(("seq", "exp"), None),
        P(("seq", "exp"), None, None),
        P(("seq", "exp"), None, None),
    )
    out_specs = (P(("seq", "exp"), None), P(("seq", "exp"), None))
    return jax.shard_map(body, mesh=mesh, in_specs=in_specs, out_specs=out_specs, check_vma=False)
```

```python
import jax
import jax.numpy as jnp
from jax import lax
from jax.experimental import pallas as pl
from jax.experimental.pallas import tpu as pltpu
from jax.sharding import PartitionSpec as P

D = 2048
HALF = D // 2
P_SIZE = 64
N = 128
Q = 256
F = 768
CAP = 12
SLAB = 2 * CAP

f32 = jnp.float32
bf16 = jnp.bfloat16
epsilon = 1e-05
LOG2_E = 1.4426950408889634


def params(mib):
    return pltpu.CompilerParams(
        dimension_semantics=("arbitrary",), vmem_limit_bytes=mib * 2**20
    )


def cost(flops, nbytes, transcendentals=0):
    return pl.CostEstimate(
        flops=int(flops), bytes_accessed=int(nbytes), transcendentals=int(transcendentals)
    )


def iota(shape, axis, kind=jnp.int32):
    return lax.broadcasted_iota(jnp.int32, shape, axis).astype(kind)


def dot(a, b):
    return jnp.dot(a, b, preferred_element_type=f32)


def dot_first(a, b):
    return lax.dot_general(a, b, (((0,), (0,)), ((), ())), preferred_element_type=f32)


def dot_last(a, b):
    return lax.dot_general(a, b, (((1,), (1,)), ((), ())), preferred_element_type=f32)


def running_sum(rates):
    heads, count = rates.shape
    upper = (iota((count, count), 0) <= iota((count, count), 1)).astype(f32).astype(bf16)
    terms = []
    for _ in range(3):
        term = rates.astype(bf16)
        terms.append(term)
        rates = rates - term.astype(f32)
    sums = dot(jnp.concatenate(terms, axis=0), upper)
    return sums[:heads] + (sums[heads : 2 * heads] + sums[2 * heads :])


def per_channel(values):
    heads = values.shape[0]
    lanes = heads * P_SIZE
    first = iota((heads, lanes), 0) * P_SIZE
    lane = iota((heads, lanes), 1)
    spread = ((lane >= first) & (lane < first + P_SIZE)).astype(f32)
    coarse = values.astype(bf16).astype(f32)
    terms = jnp.concatenate([coarse, values - coarse], axis=0).astype(bf16)
    return dot_first(terms, jnp.concatenate([spread, spread], axis=0).astype(bf16))


def row_per_channel(column):
    return per_channel(jnp.broadcast_to(column, (column.shape[0], 128)))[0:1]


def local_state_kernel(
    hidden_ref,
    gain_ref,
    value_ref,
    state_ref,
    decay_ref,
    step_ref,
    mixed_ref,
    x_ref,
    maps_ref,
    enter_ref,
    sent_ref,
    state,
    total,
):
    block = pl.program_id(0)

    @pl.when(block == 0)
    def _():
        state[...] = jnp.zeros_like(state)
        total[...] = jnp.zeros_like(total)

    wide = hidden_ref[...].astype(f32)
    scale = lax.rsqrt(jnp.mean(wide * wide, axis=-1, keepdims=True) + epsilon)
    mixed = (wide * scale * gain_ref[...]).astype(bf16)
    mixed_ref[...] = mixed
    x = dot(mixed, value_ref[...]).astype(bf16)
    x_ref[...] = x
    maps = dot(mixed, state_ref[...]).astype(bf16)
    maps_ref[...] = maps
    sums = running_sum(decay_ref[...])
    end = sums[:, Q - 1 : Q]
    weight = per_channel(jnp.exp(end - sums) * step_ref[...])
    weighted = (x.astype(f32) * weight).astype(bf16)
    old = state[...]
    enter_ref[0] = old.astype(bf16)
    new = old * row_per_channel(jnp.exp(end)) + dot_first(maps[:, :N], weighted)
    state[...] = new
    total[...] = total[...] + end

    @pl.when(block == pl.num_programs(0) - 1)
    def _():
        parts = sent_ref.shape[0]
        channels = new.shape[1]
        log_total = row_per_channel(total[:, 0:1])
        coarse = log_total.astype(bf16).astype(f32)
        which = iota((8, channels), 0)
        tail = jnp.where(which == 0, coarse, jnp.where(which == 1, log_total - coarse, 0.0))
        rows = new.reshape(parts, N // parts, channels)
        sent_ref[...] = jnp.concatenate(
            [rows, jnp.broadcast_to(tail[None], (parts, 8, channels))], axis=1
        ).astype(bf16)


def prefix_kernel(got_ref, out_ref):
    count = got_ref.shape[0]
    rows = out_ref.shape[1]
    carry = jnp.zeros(out_ref.shape[1:], f32)
    for shard in range(count):
        out_ref[shard] = carry.astype(bf16)
        got = got_ref[shard].astype(f32)
        decay = jnp.exp(got[rows : rows + 1] + got[rows + 1 : rows + 2])
        carry = decay * carry + got[:rows]


def within_kernel(
    mixed_ref,
    gate_w_ref,
    x_ref,
    maps_ref,
    decay_ref,
    step_ref,
    enter_ref,
    skip_ref,
    *rest,
):
    gate_ref, within_ref = rest[-2:]
    gate_ref[...] = dot(mixed_ref[...], gate_w_ref[...]).astype(bf16)
    sums = running_sum(decay_ref[...])
    heads = sums.shape[0]
    maps = maps_ref[...]
    part = Q // 2
    scores = dot_last(maps[:, N:], maps[:, :N])
    from_start = per_channel(jnp.exp(sums)) * dot(maps[:, N:], enter_ref[0])
    scaled = sums * LOG2_E
    source = scaled - jnp.log2(step_ref[...])
    blank = jnp.zeros((128 - heads, Q), f32)
    target = jnp.concatenate([scaled, blank], axis=0).T
    causal = iota((part, part), 0) >= iota((part, part), 1)
    left = (iota((Q, 2 * P_SIZE), 1) < P_SIZE).astype(f32).astype(bf16)
    right = (iota((Q, 2 * P_SIZE), 1) >= P_SIZE).astype(f32).astype(bf16)
    for pair in range(heads // 2):
        top, bottom = [], []
        for head in (2 * pair, 2 * pair + 1):
            column = target[:, head : head + 1]
            row = source[head : head + 1]
            corner = jnp.where(causal, column[:part] - row[:, :part], -jnp.inf)
            top.append((scores[:part, :part] * jnp.exp2(corner)).astype(bf16))
            past = column[part:] - row[:, :part]
            bottom.append((scores[part:, :part] * jnp.exp2(past)).astype(bf16))
            corner = jnp.where(causal, column[part:] - row[:, part:], -jnp.inf)
            bottom.append((scores[part:, part:] * jnp.exp2(corner)).astype(bf16))
        lanes = slice(pair * 2 * P_SIZE, (pair + 1) * 2 * P_SIZE)
        x = x_ref[:, lanes]
        x_left, x_right = x * left, x * right
        skip = x.astype(f32) * skip_ref[:, lanes] + from_start[:, lanes]
        within_ref[:part, lanes] = skip[:part] + dot(
            jnp.concatenate(top, axis=1),
            jnp.concatenate([x_left[:part], x_right[:part]], axis=0),
        )
        within_ref[part:, lanes] = skip[part:] + dot(
            jnp.concatenate(bottom, axis=1), jnp.concatenate([x_left, x_right], axis=0)
        )


def normed_kernel(
    core_ref,
    within_ref,
    maps_ref,
    gate_ref,
    decay_ref,
    incoming_ref,
    gain_ref,
    own_ref,
    other_ref,
    before,
):
    block = pl.program_id(0)

    @pl.when(block == 0)
    def _():
        before[...] = jnp.zeros_like(before)

    sums = running_sum(decay_ref[...]) + before[:, 0:1]
    before[...] = jnp.broadcast_to(sums[:, Q - 1 : Q], before.shape)
    carried = per_channel(jnp.exp(sums)) * dot(maps_ref[...], incoming_ref[...])
    gate = gate_ref[...].astype(f32)
    gated = (within_ref[...] + carried) * (gate * jax.nn.sigmoid(gate))
    scale = lax.rsqrt(jnp.mean(gated * gated, axis=-1, keepdims=True) + epsilon)
    normed = gated * scale * gain_ref[...]
    rows = own_ref.shape[0]
    first, second = normed[:rows], normed[rows:]
    mine = core_ref[0] == 0
    own_ref[...] = jnp.where(mine, first, second).astype(bf16)
    other_ref[...] = jnp.where(mine, second, first).astype(bf16)


def own_part_kernel(at_ref, own_ref, own_w_ref, got_w_ref, part_ref, kept_ref, ready):
    keep = pltpu.make_async_copy(got_w_ref, kept_ref, ready)
    keep.start()
    part_ref[...] = dot(own_ref[...], own_w_ref[...])
    keep.wait()


def finish_kernel(at_ref, part_ref, got_ref, got_w_ref, left_ref, right_ref):
    out = part_ref[...] + dot(got_ref[...], got_w_ref[...])
    left_ref[...] = out[:, :HALF].astype(bf16)
    right_ref[...] = out[:, HALF:].astype(bf16)


def halves_kernel(
    at_ref, own_a_ref, got_a_ref, own_b_ref, got_b_ref, own_w_ref, got_w_ref, *rest
):
    *more, a_ref, b_ref = rest
    halves = (slice(0, HALF), slice(HALF, D))
    if not more:
        halves = halves[::-1]
    a = dot(own_a_ref[...], own_w_ref[:, halves[0]]) + dot(got_a_ref[...], got_w_ref[:, halves[0]])
    b = dot(own_b_ref[...], own_w_ref[:, halves[1]]) + dot(got_b_ref[...], got_w_ref[:, halves[1]])
    if more:
        a = a + more[0][...].astype(f32)
        b = b + more[1][...].astype(f32)
    a_ref[...] = a.astype(bf16)
    b_ref[...] = b.astype(bf16)


def slots(row):
    place = row - SLAB * jnp.floor((row + 0.5) * (1.0 / SLAB))
    slot = jnp.where(place < 8, place, jnp.where(place < 20, place - 8, place - 12))
    second = ((place >= 8) & (place < 16)) | (place >= 20)
    return slot, second


def expert_of(block, rows, experts):
    gap = iota((rows, experts), 0) + block * rows - SLAB * iota((rows, experts), 1)
    return ((gap >= 0) & (gap < SLAB)).astype(f32).astype(bf16)


def route_kernel(ids_ref, named_ref, rank_ref, picker_ref, ranks):
    block = pl.program_id(0)
    tokens, experts = named_ref.shape

    @pl.when(block == 0)
    def _():
        lane = iota((tokens, experts), 1)
        named = jnp.zeros((tokens, experts), f32)
        for k in range(ids_ref.shape[1]):
            named = named + (ids_ref[:, k : k + 1] == lane).astype(f32)
        named_ref[...] = named
        earlier = (iota((tokens, tokens), 0) > iota((tokens, tokens), 1)).astype(f32)
        rank = dot(earlier.astype(bf16), named.astype(bf16))
        rank = jnp.where(named > 0.5, rank, -1.0)
        rank_ref[...] = rank
        ranks[...] = rank.astype(bf16)

    rows = picker_ref.shape[0]
    ranked = dot_last(expert_of(block, rows, experts), ranks[...])
    slot, second = slots(iota((rows, tokens), 0, f32))
    hit = (ranked == slot).astype(f32)
    picker_ref[:, :tokens] = jnp.where(second, 0.0, hit).astype(bf16)
    picker_ref[:, tokens:] = jnp.where(second, hit, 0.0).astype(bf16)


def dispatch_kernel(
    where_ref,
    left_a_ref,
    left_b_ref,
    left_c_ref,
    right_a_ref,
    right_b_ref,
    right_c_ref,
    hidden_ref,
    gain_ref,
    router_ref,
    named_ref,
    picker_ref,
    mixer_ref,
    weight_ref,
    out_ref,
):
    left = left_a_ref[...].astype(f32) + left_b_ref[...].astype(f32)
    right = right_a_ref[...].astype(f32) + right_b_ref[...].astype(f32)
    head_sum = jnp.concatenate(
        [left + left_c_ref[...].astype(f32), right + right_c_ref[...].astype(f32)], axis=1
    )
    mixer_out = (hidden_ref[...].astype(f32) + head_sum).astype(bf16)
    mixer_ref[...] = mixer_out
    wide = mixer_out.astype(f32)
    scale = lax.rsqrt(jnp.mean(wide * wide, axis=-1, keepdims=True) + epsilon)
    expert_input = (wide * scale * gain_ref[...]).astype(bf16)
    rows_in = jnp.concatenate([expert_input[:, :HALF], expert_input[:, HALF:]], axis=0)
    picked = named_ref[...] * jax.nn.sigmoid(dot(expert_input, router_ref[...]))
    weight_ref[...] = picked / jnp.sum(picked, axis=-1, keepdims=True)
    step = out_ref.shape[0] // 8
    for i in range(8):
        part = slice(i * step, (i + 1) * step)
        out_ref[part] = dot(picker_ref[part], rows_in).astype(bf16)


def expert_kernel(got_ref, up_ref, down_ref, out_ref):
    peers = out_ref.shape[0]
    group = pl.ds(pl.program_id(0) * peers, peers)
    rows = peers * 8
    part = rows // 2
    place = iota((rows, rows), 0)
    lane = iota((rows, rows), 1)

    def source(row):
        inner = row & (part - 1)
        return ((inner >> 2) << 3) + jnp.where(row >= part, 4, 0) + (inner & 3)

    apart = (source(place) == lane).astype(f32).astype(bf16)
    together = (place == source(lane)).astype(f32).astype(bf16)
    tail = dot(apart, got_ref[group, 2].reshape(rows, HALF)).astype(bf16)
    x0 = jnp.concatenate([got_ref[group, 0].reshape(rows, HALF), tail[:part]], axis=0)
    x1 = jnp.concatenate([got_ref[group, 1].reshape(rows, HALF), tail[part:]], axis=0)
    projected = dot(x0, up_ref[0, :HALF]) + dot(x1, up_ref[0, HALF:])
    gate = projected[:, :F]
    hidden = (gate * jax.nn.sigmoid(gate) * projected[:, F:]).astype(bf16)
    y0 = dot(hidden, down_ref[0, :, :HALF]).astype(bf16)
    y1 = dot(hidden, down_ref[0, :, HALF:]).astype(bf16)
    out_ref[:, 0] = y0[:rows].reshape(peers, 8, HALF)
    out_ref[:, 1] = y1[:rows].reshape(peers, 8, HALF)
    tail = jnp.concatenate([y0[rows:], y1[rows:]], axis=0)
    out_ref[:, 2] = dot(together, tail).astype(bf16).reshape(peers, 8, HALF)


def combine_weight_kernel(rank_ref, weight_ref, out_ref):
    block = pl.program_id(0)
    tokens, experts = rank_ref.shape
    rows = out_ref.shape[1]
    member = expert_of(block, rows, experts)
    ranked = dot_last(rank_ref[...].astype(bf16), member)
    weight = dot_last(weight_ref[...].astype(bf16), member)
    slot, second = slots(iota((tokens, rows), 1, f32))
    weight = jnp.where(ranked == slot, weight, 0.0)
    out_ref[:tokens] = jnp.where(second, 0.0, weight).astype(bf16)
    out_ref[tokens:] = jnp.where(second, weight, 0.0).astype(bf16)


def combine_kernel(got_ref, weight_ref, mixer_ref, out_ref, held, ready):
    tokens = mixer_ref.shape[0]
    parts, group = held.shape[0], held.shape[1]
    rows = group * SLAB

    def fetch(i):
        return pltpu.make_async_copy(
            got_ref.at[pl.ds(i * group, group)], held.at[i], ready.at[i]
        )

    ahead = 3
    for i in range(ahead):
        fetch(i).start()
    total = jnp.zeros((2 * tokens, HALF), f32)
    for i in range(parts):
        fetch(i).wait()
        if i + ahead < parts:
            fetch(i + ahead).start()
        total += dot(weight_ref[:, i * rows : (i + 1) * rows], held[i].reshape(rows, HALF))
    out_ref[:, :HALF] = (mixer_ref[:, :HALF].astype(f32) + total[:tokens]).astype(bf16)
    out_ref[:, HALF:] = (mixer_ref[:, HALF:].astype(f32) + total[tokens:]).astype(bf16)


def fixed(*shape):
    return pl.BlockSpec(shape, lambda *_: (0,) * len(shape))


def fixed_once(*shape):
    return pl.BlockSpec(
        shape, lambda *_: (0,) * len(shape), pipeline_mode=pl.Buffered(1)
    )


def by_rows(*shape):
    rest = (0,) * (len(shape) - 1)
    return pl.BlockSpec(shape, lambda i, *_: (i, *rest))


def by_lanes(*shape):
    return pl.BlockSpec(shape, lambda i, *_: (0, i))


def resident():
    return pl.BlockSpec(memory_space=pltpu.VMEM)


def shape_of(kind, *shape):
    return jax.ShapeDtypeStruct(shape, kind)


def stored(kind, *shape):
    return pltpu.HBM(shape, kind)


def from_hbm(*arrays):
    return [pltpu.with_memory_space_constraint(a, pltpu.HBM) for a in arrays]


def from_vmem(*arrays):
    return [pltpu.with_memory_space_constraint(a, pltpu.VMEM) for a in arrays]


def body(
    hidden,
    mixer_gain,
    gate_proj,
    value_proj,
    state_proj,
    log_decay,
    step_size,
    skip_gain,
    group_gain,
    out_proj,
    moe_gain,
    router,
    expert_ids,
    expert_gate_up,
    expert_down,
):
    rows = hidden.shape[0]
    heads = log_decay.shape[1]
    channels = heads * P_SIZE
    blocks = rows // Q
    seq_count = lax.axis_size("seq")
    exp_count = lax.axis_size("exp")
    peers = seq_count * exp_count
    place = lax.axis_index("exp")
    core, line = place % 2, place // 2
    lines = exp_count // 2
    own_rows = rows // exp_count
    slice_rows = N // seq_count
    experts = router.shape[1]
    slab_rows = experts * SLAB
    per_step = slab_rows // 4

    swap = [(i, i ^ 1) for i in range(exp_count)]
    other_proj = lax.ppermute(out_proj, "exp", swap)
    decay = log_decay.T
    step = step_size.T

    mixed, x, maps, enter, sent = pl.pallas_call(
        local_state_kernel,
        grid=(blocks,),
        in_specs=[
            by_rows(Q, D),
            fixed(1, D),
            fixed_once(D, channels),
            fixed_once(D, 2 * N),
            by_lanes(heads, Q),
            by_lanes(heads, Q),
        ],
        out_specs=[
            by_rows(Q, D),
            by_rows(Q, channels),
            by_rows(Q, 2 * N),
            by_rows(1, N, channels),
            fixed(seq_count, slice_rows + 8, channels),
        ],
        out_shape=[
            stored(bf16, rows, D),
            stored(bf16, rows, channels),
            stored(bf16, rows, 2 * N),
            stored(bf16, blocks, N, channels),
            shape_of(bf16, seq_count, slice_rows + 8, channels),
        ],
        scratch_shapes=[pltpu.VMEM((N, channels), f32), pltpu.VMEM((heads, 128), f32)],
        compiler_params=params(24),
        cost_estimate=cost(2 * rows * D * (channels + 2 * N), 16 * 2**20),
        name="local_state",
    )(*from_hbm(hidden, mixer_gain.reshape(1, D), value_proj, state_proj, decay, step))

    slices = lax.all_to_all(sent, "seq", split_axis=0, concat_axis=0, tiled=True)

    gate_w = from_vmem(gate_proj)
    inside = from_hbm(mixed, x, maps, decay, step, enter)
    skip = jnp.repeat(skip_gain, P_SIZE).reshape(1, channels)
    half_blocks = blocks // 2

    def within_half(first, earlier):
        def block(*shape):
            return pl.BlockSpec(shape, lambda i: (i + first, *(0,) * (len(shape) - 1)))

        def lanes():
            return pl.BlockSpec((heads, Q), lambda i: (0, i + first))

        mixed, x, maps, decay, step, enter = inside
        return pl.pallas_call(
            within_kernel,
            grid=(half_blocks,),
            in_specs=[
                block(Q, D),
                resident(),
                block(Q, channels),
                block(Q, 2 * N),
                lanes(),
                lanes(),
                block(1, N, channels),
                fixed(1, channels),
            ]
            + [pl.BlockSpec(memory_space=pl.ANY)] * len(earlier),
            out_specs=[block(Q, channels), block(Q, channels)],
            out_shape=[stored(bf16, rows, channels), stored(f32, rows, channels)],
            input_output_aliases={8 + i: i for i in range(len(earlier))},
            compiler_params=params(20),
            cost_estimate=cost(rows * channels * (D + 2 * Q), 5 * 2**20, rows * Q * heads // 2),
            name="within",
        )(mixed, *gate_w, x, maps, decay, step, enter, skip, *earlier)

    gate, within = within_half(0, ())
    slices, gate, within = lax.optimization_barrier((slices, gate, within))

    before = pl.pallas_call(
        prefix_kernel,
        out_shape=shape_of(bf16, seq_count, slice_rows, channels),
        compiler_params=pltpu.CompilerParams(vmem_limit_bytes=8 * 2**20),
        name="prefix",
    )(slices)
    incoming = lax.all_to_all(before, "seq", split_axis=0, concat_axis=0, tiled=True)
    incoming = incoming.reshape(N, channels)

    gate, within = within_half(half_blocks, from_hbm(gate, within))
    incoming, gate, within = lax.optimization_barrier((incoming, gate, within))

    own, other = pl.pallas_call(
        normed_kernel,
        grid_spec=pltpu.PrefetchScalarGridSpec(
            num_scalar_prefetch=1,
            grid=(blocks,),
            in_specs=[
                by_rows(Q, channels),
                pl.BlockSpec((Q, N), lambda i, *_: (i, 1)),
                by_rows(Q, channels),
                by_lanes(heads, Q),
                fixed(N, channels),
                fixed(1, channels),
            ],
            out_specs=[by_rows(own_rows, channels), by_rows(own_rows, channels)],
            scratch_shapes=[pltpu.VMEM((heads, 128), f32)],
        ),
        out_shape=[shape_of(bf16, rows // 2, channels)] * 2,
        compiler_params=params(12),
        cost_estimate=cost(2 * rows * N * channels, 5 * 2**20),
        name="normed",
    )(
        core.reshape(1),
        *from_hbm(within, maps, gate, decay),
        incoming,
        group_gain.reshape(1, channels),
    )
    got = lax.ppermute(other, "exp", swap)

    at = jnp.stack([(line + hop) % lines for hop in range(lines)])

    def rows_of(hop):
        return pl.BlockSpec((own_rows, channels), lambda i, at: (at[hop], 0))

    def project(kernel, in_specs, out_specs, out_shape, share, name, scratch=()):
        return pl.pallas_call(
            kernel,
            grid_spec=pltpu.PrefetchScalarGridSpec(
                num_scalar_prefetch=1,
                grid=(1,),
                in_specs=in_specs,
                out_specs=out_specs,
                scratch_shapes=scratch,
            ),
            out_shape=out_shape,
            compiler_params=params(10),
            cost_estimate=cost(share * own_rows * channels * D, 3 * 2**20),
            name=name,
        )

    half = fixed(own_rows, HALF)
    half_pair = [shape_of(bf16, own_rows, HALF)] * 2

    own_w = from_vmem(out_proj)
    part, got_w = project(
        own_part_kernel,
        [rows_of(2), resident(), pl.BlockSpec(memory_space=pl.ANY)],
        [fixed(own_rows, D), resident()],
        [pltpu.VMEM((own_rows, D), f32), pltpu.VMEM((channels, D), bf16)],
        2,
        "own_part",
        [pltpu.SemaphoreType.DMA],
    )(at, own, *own_w, *from_hbm(other_proj))
    got, part = lax.optimization_barrier((got, part))
    projections = own_w + from_vmem(got_w)

    def halves(at, hop_a, hop_b, *arrived, kept=half_pair):
        return project(
            halves_kernel,
            [rows_of(hop_a), rows_of(hop_a), rows_of(hop_b), rows_of(hop_b)]
            + [resident(), resident()]
            + [half] * len(arrived),
            [half, half],
            kept,
            4,
            "halves",
        )(at, own, got, own, got, *projections, *arrived)

    def send(piece, hop):
        moves = [(i, (i + 2 * hop) % exp_count) for i in range(exp_count)]
        return lax.ppermute(piece, "exp", moves)

    far_left, far_right = project(
        finish_kernel,
        [fixed(own_rows, D), rows_of(2), resident()],
        [half, half],
        half_pair,
        2,
        "finish",
    )(at, part, got, projections[1])
    via_next, via_last = send(far_left, 1), send(far_right, 3)
    next_right, last_left = halves(at, 1, 3)
    later_at, _ = lax.optimization_barrier((at, next_right))
    mine_right, mine_left = from_hbm(
        *halves(later_at, 0, 0, kept=[stored(bf16, own_rows, HALF)] * 2)
    )
    next_right, last_left, mine_left, mine_right = lax.optimization_barrier(
        (next_right, last_left, mine_left, mine_right)
    )
    right_pieces = [send(next_right, 1), mine_right]
    left_pieces = [send(last_left, 3), mine_left]
    next_left, last_right = halves(at, 1, 3, via_next, via_last)
    left_pieces.append(send(next_left, 1))
    right_pieces.append(send(last_right, 3))
    late_ids, _ = lax.optimization_barrier((expert_ids, next_left))
    named, rank, picker = pl.pallas_call(
        route_kernel,
        grid=(4,),
        in_specs=[fixed(own_rows, expert_ids.shape[1])],
        out_specs=[
            fixed(own_rows, experts),
            fixed(own_rows, experts),
            by_rows(per_step, 2 * own_rows),
        ],
        out_shape=[
            shape_of(f32, own_rows, experts),
            shape_of(f32, own_rows, experts),
            pltpu.VMEM((slab_rows, 2 * own_rows), bf16),
        ],
        scratch_shapes=[pltpu.VMEM((own_rows, experts), bf16)],
        compiler_params=params(12),
        cost_estimate=cost(2 * slab_rows * experts * own_rows, 4 * 2**20),
        name="route",
    )(late_ids)

    mixer_out, weight, outgoing = pl.pallas_call(
        dispatch_kernel,
        grid_spec=pltpu.PrefetchScalarGridSpec(
            num_scalar_prefetch=1,
            grid=(1,),
            in_specs=[resident()] * 6
            + [
                pl.BlockSpec((own_rows, D), lambda i, at: (at[0], 0)),
                fixed(1, D),
                fixed(D, experts),
                resident(),
                resident(),
            ],
            out_specs=[fixed(own_rows, D), fixed(own_rows, experts), resident()],
        ),
        out_shape=[
            shape_of(bf16, own_rows, D),
            shape_of(f32, own_rows, experts),
            pltpu.VMEM((slab_rows, HALF), bf16),
        ],
        compiler_params=params(24),
        cost_estimate=cost(4 * slab_rows * own_rows * HALF, 10 * 2**20),
        name="dispatch",
    )(
        place.reshape(1),
        *left_pieces,
        *right_pieces,
        *from_hbm(hidden, moe_gain.reshape(1, D), router),
        named,
        *from_vmem(picker),
    )

    arrived = lax.all_to_all(
        outgoing.reshape(peers, SLAB, HALF),
        ("seq", "exp"),
        split_axis=0,
        concat_axis=0,
        tiled=True,
    ).reshape(peers, 3, 8, HALF)
    group = peers // 4
    combine_weight = pl.pallas_call(
        combine_weight_kernel,
        grid=(4,),
        in_specs=[fixed(own_rows, experts), fixed(own_rows, experts)],
        out_specs=by_lanes(2 * own_rows, per_step),
        out_shape=pltpu.VMEM((2 * own_rows, slab_rows), bf16),
        compiler_params=params(12),
        cost_estimate=cost(4 * slab_rows * experts * own_rows, 4 * 2**20),
        name="combine_weight",
    )(rank, weight)

    results = pl.pallas_call(
        expert_kernel,
        grid=(4,),
        in_specs=[resident()] * 3,
        out_specs=by_rows(group, 3, 8, HALF),
        out_shape=stored(bf16, peers, 3, 8, HALF),
        compiler_params=params(28),
        cost_estimate=cost(6 * peers * CAP * D * F, 22 * 2**20, peers * CAP * F),
        name="experts",
    )(*from_vmem(arrived, expert_gate_up, expert_down))
    returned = lax.all_to_all(
        results.reshape(peers, SLAB, HALF),
        ("seq", "exp"),
        split_axis=0,
        concat_axis=0,
        tiled=True,
    )

    layer_out = pl.pallas_call(
        combine_kernel,
        in_specs=[pl.BlockSpec(memory_space=pl.ANY), resident(), resident()],
        out_specs=resident(),
        out_shape=shape_of(bf16, own_rows, D),
        scratch_shapes=[
            pltpu.VMEM((8, peers // 8, SLAB, HALF), bf16),
            pltpu.SemaphoreType.DMA((8,)),
        ],
        compiler_params=pltpu.CompilerParams(vmem_limit_bytes=24 * 2**20),
        cost_estimate=cost(4 * slab_rows * own_rows * HALF, 8 * 2**20),
        name="combine",
    )(*from_hbm(returned), *from_vmem(combine_weight, mixer_out))
    return (mixer_out, layer_out)


def solution(mesh):
    in_specs = (
        P("seq", None),
        P(),
        P(None, "exp"),
        P(None, "exp"),
        P(None, "exp"),
        P("seq", "exp"),
        P("seq", "exp"),
        P("exp"),
        P("exp"),
        P("exp", None),
        P(),
        P(),
        P(("seq", "exp"), None),
        P(("seq", "exp"), None, None),
        P(("seq", "exp"), None, None),
    )
    out_specs = (P(("seq", "exp"), None), P(("seq", "exp"), None))
    return jax.shard_map(body, mesh=mesh, in_specs=in_specs, out_specs=out_specs, check_vma=False)
```
